32 devices in a mesh: parts: 2 (over y), space: 8 (over z, x), tm: 2 (over core).
Axes of the slice: x: 2, y: 2, z: 4, core: 2. Of those that a mesh axis runs over, the one named last changes fastest.
Arguments:
- eigvecs: bfloat16 [4, 2, 256, 3, 1728], P(('parts', 'tm'), None, None, None, 'space'), parts along dimension 0, may hold values from -1.25 to 1.25
- links: bfloat16 [4, 3, 3, 3, 2, 1728], P(('parts', 'tm'), None, None, None, None, 'space'), parts along dimension 0, may hold values from -2.5 to 2.5
- dirs: int32 [3], replicated, may hold values from 0 to 2, each once
- peram: bfloat16 [4, 2, 1024, 1024], P(('parts', 'tm'), None, 'space'), parts along dimension 0, may hold values from -0.25 to 0.25
Outputs:
- meson_blocks: bfloat16 [4, 3, 2, 1024, 1024], P(('parts', 'tm'), None, None, 'space'), parts along dimension 0
The draws below stay inside these ranges and needn't reach their ends.
There are 2 independent parts, one for each index of `parts`. The reference program is written for one: setup_inputs(seed, part) draws one part's arguments, and reference() takes and returns one part's arrays. A program takes and returns all parts, laid end to end along the dimension named above; an argument that names none is the same for every part. Nothing has to cross between parts.
All inputs are finite; a program needn't handle non-finite values.
Results may differ from the reference program's by a relative error of at most 0.0061.
Values may be sent and summed in bfloat16 or wider, within the bound.
No kernel may reach another device: no remote copies, remote signals or barrier semaphores. Data moves between devices by JAX's collectives and lax.ppermute only.
A program may use at most 64 MiB of HBM per device.

```python
import jax
import jax.numpy as jnp
from jax import lax

K = 256
SPIN = 4
NDIR = 3
TS = 1
LX = 9
LZ = 24
LY = 8
SITES = 1728
NT = 2


def level_of(rng, shape, pieces, low, high):
    factor_of = 1.0
    for dim, shards_of in pieces:
        draws = jax.random.uniform(jax.random.fold_in(jax.random.fold_in(rng, 6), dim), (shards_of,), jnp.float32, low / len(pieces), high / len(pieces))
        factor_of = factor_of * jnp.repeat(jnp.exp(draws), shape[dim] // shards_of).reshape((-1,) + (1,) * (len(shape) - 1 - dim))
    return factor_of


def centred(own_key, dims, deviation, limit, cuts=(), kind=jnp.bfloat16):
    loudness = level_of(own_key, dims, cuts, -0.22, 0.18) if cuts else 1.0
    values = jax.random.normal(own_key, dims, jnp.float32) * deviation * loudness
    return jnp.minimum(jnp.maximum(values, -limit), limit).astype(kind)


def setup_inputs(seed: int = 0, part: int = 0) -> dict:
    key_of = jax.random.split(jax.random.key(seed), 5)
    part_keys = jax.random.split(jax.random.fold_in(key_of[4], part), 5)
    return {
        "eigvecs": centred(part_keys[0], (NT, 2, K, 3, SITES), (0.85 * (6 * SITES) ** -0.25), 1.25, ((0, 2), (4, 8))),
        "links": centred(part_keys[1], (NT, 3, 3, 3, 2, SITES), 0.4, 2.5, ((0, 2), (5, 8))),
        "dirs": jax.random.permutation(key_of[2], 3).astype(jnp.int32),
        "peram": centred(part_keys[3], (NT, 2, K * SPIN, K * SPIN), (2 * K) ** -0.5, 0.25, ((0, 2), (2, 8))),
    }


def to_lattice(values):
    return values.reshape(values.shape[:-1] + (LY, LX, LZ))


def link_apply(link_mat, values_in, adjoint):
    real_rows = []
    imag_rows = []
    for out_row in range(3):
        real_sum = jnp.zeros(values_in.shape[1:2] + values_in.shape[3:], jnp.float32)
        imag_sum = jnp.zeros(values_in.shape[1:2] + values_in.shape[3:], jnp.float32)
        for in_col in range(3):
            if adjoint:
                link_entry = link_mat[in_col, out_row]
                conj_sign = -1.0
            else:
                link_entry = link_mat[out_row, in_col]
                conj_sign = 1.0
            link_real = link_entry[0].astype(jnp.float32)[None]
            link_imag = (conj_sign * link_entry[1].astype(jnp.float32))[None]
            vec_real = values_in[0, :, in_col].astype(jnp.float32)
            vec_imag = values_in[1, :, in_col].astype(jnp.float32)
            real_sum = real_sum + link_real * vec_real - link_imag * vec_imag
            imag_sum = imag_sum + link_real * vec_imag + link_imag * vec_real
        real_rows.append(real_sum)
        imag_rows.append(imag_sum)
    return jnp.stack([jnp.stack(real_rows, axis=1), jnp.stack(imag_rows, axis=1)])


def neighbour(values_in, direction, step_size):
    lattice_axis = (-2, -3, -1)[direction]
    return jnp.roll(values_in, -step_size, axis=lattice_axis)


def contract(left, right):
    return lax.dot_general(left, right, (((1,), (1,)), ((), ())), preferred_element_type=jnp.float32)


def elemental(eigen_field, derivative):
    vectors = eigen_field.shape[1]
    vec_real = eigen_field[0].reshape(vectors, -1)
    vec_imag = eigen_field[1].reshape(vectors, -1)
    der_real = derivative[0].reshape(vectors, -1)
    der_imag = derivative[1].reshape(vectors, -1)
    return jnp.stack([contract(vec_real, der_real) + contract(vec_imag, der_imag),
                      contract(vec_real, der_imag) - contract(vec_imag, der_real)])


def reference(eigvecs, links, dirs, peram):
    choose = dirs[:, None] == jnp.arange(3, dtype=jnp.int32)[None, :]
    columns = peram.shape[2]
    groups = NT // TS
    results = []
    for time_slice in range(NT):
        eigen_field = to_lattice(eigvecs[time_slice])
        links_now = to_lattice(links[time_slice])
        elementals = []
        for direction in range(3):
            back_term = link_apply(links_now[direction], eigen_field, True).astype(jnp.bfloat16)
            ahead_term = link_apply(links_now[direction], neighbour(eigen_field, direction, 1), False)
            derivative = (ahead_term - neighbour(back_term, direction, -1).astype(jnp.float32)).astype(jnp.bfloat16)
            elementals.append(elemental(eigen_field, derivative))
        elementals = jnp.stack(elementals)
        picked = jnp.sum(jnp.where(choose[:, :, None, None, None], elementals[None], 0.0), axis=1)
        elem_low = picked.astype(jnp.bfloat16)
        partner_slice = ((time_slice // TS + 1) % groups) * TS + time_slice % TS
        peram_block = peram[partner_slice]
        elem_real = elem_low[:, 0].astype(jnp.float32)
        elem_imag = elem_low[:, 1].astype(jnp.float32)
        peram_real = peram_block[0].astype(jnp.float32).reshape(columns, K, SPIN)
        peram_imag = peram_block[1].astype(jnp.float32).reshape(columns, K, SPIN)
        highest = lax.Precision.HIGHEST
        out_real = (jnp.einsum('jkl,cls->jcks', elem_real, peram_real, precision=highest)
                    - jnp.einsum('jkl,cls->jcks', elem_imag, peram_imag, precision=highest))
        out_imag = (jnp.einsum('jkl,cls->jcks', elem_real, peram_imag, precision=highest)
                    + jnp.einsum('jkl,cls->jcks', elem_imag, peram_real, precision=highest))
        stacked = jnp.stack([out_real, out_imag], axis=1)
        results.append(stacked.reshape(NDIR, 2, columns, K * SPIN).astype(jnp.bfloat16))
    return jnp.stack(results)
```

```python
import functools

import jax
import jax.numpy as jnp
from jax import lax
from jax.experimental import pallas as pl
from jax.experimental.pallas import tpu as pltpu
from jax.sharding import PartitionSpec as P

SPIN = 4
LX = 9
LZ = 24
F32 = jnp.float32
BF16 = jnp.bfloat16
VMEM = pl.BlockSpec(memory_space=pltpu.VMEM)


def half_rows(sites):
    return 8 * ((sites + 15) // 16)


def padded(count):
    return 8 * ((count + 7) // 8)


def identity(size):
    rows = lax.broadcasted_iota(jnp.int32, (size, size), 0)
    cols = lax.broadcasted_iota(jnp.int32, (size, size), 1)
    return jnp.where(rows == cols, 1.0, 0.0).astype(BF16)


def dot(left, right, left_dim, right_dim):
    return lax.dot_general(
        left, right, (((left_dim,), (right_dim,)), ((), ())), preferred_element_type=F32
    )


def adjoint_product(columns, base, vec):
    real_rows, imag_rows = [], []
    for out in range(3):
        real_sum = imag_sum = None
        for inner in range(3):
            at = base + (inner * 3 + out) * 2
            link_real = columns[:, at : at + 1]
            link_imag = columns[:, at + 1 : at + 2]
            real = link_real * vec[inner] + link_imag * vec[3 + inner]
            imag = link_real * vec[3 + inner] - link_imag * vec[inner]
            real_sum = real if real_sum is None else real_sum + real
            imag_sum = imag if imag_sum is None else imag_sum + imag
        real_rows.append(real_sum)
        imag_rows.append(imag_sum)
    return real_rows + imag_rows


def packed_elemental(w_real, w_imag, v_real, v_imag):
    real = dot(w_real, v_real, 0, 0) + dot(w_imag, v_imag, 0, 0)
    imag = dot(w_real, v_imag, 0, 0) - dot(w_imag, v_real, 0, 0)
    return (real + imag) + jnp.transpose(imag - real)


def prepare_kernel(sites, v_ref, u_ref, across_ref, along_ref):
    half = half_rows(sites)
    overlap = 2 * half - sites
    vectors = v_ref.shape[1]
    parity = lax.rem(lax.axis_index("space"), 2)
    entries = u_ref.shape[0]

    def fill(ref, upper):
        first = sites - half if upper else 0
        for comp in range(6):
            ref[pl.ds(comp * half, half), :] = v_ref[pl.ds(comp * sites + first, half), :]
        links = u_ref[:, first : first + half].astype(F32)
        if upper and overlap:
            lane = lax.broadcasted_iota(jnp.int32, links.shape, 1)
            links = jnp.where(lane < overlap, 0.0, links)
        rows = ref.shape[0] - 6 * half
        block = jnp.concatenate(
            [
                jnp.concatenate([links, jnp.zeros((rows - entries, half), F32)], axis=0),
                jnp.zeros((rows, vectors - half), F32),
            ],
            axis=1,
        )
        ref[pl.ds(6 * half, rows), :] = block.astype(BF16)

    @pl.when(parity == 0)
    def _():
        fill(across_ref, True)
        fill(along_ref, False)

    @pl.when(parity == 1)
    def _():
        fill(across_ref, False)
        fill(along_ref, True)


def front_kernel(sites, v_ref, u_ref, o_ref, w_ref):
    planes = sites // LZ
    vectors = v_ref.shape[1]
    columns = dot(identity(sites), u_ref[...], 1, 1)
    for plane in range(planes):
        slab, along = plane // LX, plane % LX
        start = plane * LZ
        vec = [v_ref[pl.ds(comp * sites + start, LZ), :].astype(F32) for comp in range(6)]
        here = columns[start : start + LZ, :]
        ahead = (slab * LX + (along + 1) % LX) * LZ
        for comp, value in enumerate(adjoint_product(here, 0, vec)):
            w_ref[0, pl.ds(comp * sites + ahead, LZ), :] = value
        for comp, value in enumerate(adjoint_product(here, 18, vec)):
            w_ref[1, pl.ds(comp * sites + start, LZ), :] = pltpu.roll(value, 1, 0)
    real = pl.ds(0, 3 * sites)
    imag = pl.ds(3 * sites, 3 * sites)
    for index in range(2):
        packed = packed_elemental(
            w_ref[index, real, :].astype(BF16),
            w_ref[index, imag, :].astype(BF16),
            v_ref[real, :],
            v_ref[imag, :],
        )
        o_ref[pl.ds(index * vectors, vectors), :] = packed.astype(BF16)


def middle_kernel(half, own_ref, across_ref, along_ref, o_ref, w_ref):
    even = lax.rem(lax.axis_index("space"), 2) == 0
    first = jnp.where(even, own_ref[...], along_ref[...])
    last = jnp.where(even, along_ref[...], own_ref[...])
    middle = across_ref[...]
    ident = identity(half)
    for index, field in enumerate((first, middle)):
        columns = dot(ident, field[6 * half :, :half], 1, 1)
        vec = [field[comp * half : (comp + 1) * half, :].astype(F32) for comp in range(6)]
        for comp, value in enumerate(adjoint_product(columns, 0, vec)):
            part, inner = comp // 3, comp % 3
            w_ref[part, pl.ds((index * 3 + inner) * half, half), :] = value
    v_real = jnp.concatenate([middle[: 3 * half], last[: 3 * half]], axis=0)
    v_imag = jnp.concatenate([middle[3 * half : 6 * half], last[3 * half : 6 * half]], axis=0)
    packed = packed_elemental(w_ref[0].astype(BF16), w_ref[1].astype(BF16), v_real, v_imag)
    o_ref[...] = packed.astype(BF16)


def spread(size):
    rows = lax.broadcasted_iota(jnp.int32, (SPIN * size, SPIN * size), 0)
    cols = lax.broadcasted_iota(jnp.int32, (SPIN * size, SPIN * size), 1)
    target = (rows % size) * SPIN + rows // size
    return jnp.where(cols == target, 1.0, 0.0).astype(BF16)


def spins_kernel(p_ref, o_ref, s_ref):
    columns, wide = p_ref.shape[1], p_ref.shape[2]
    vectors = wide // SPIN
    block = 128
    table = spread(block)
    s_ref[...] = table
    for part in range(2):
        for chunk in range(vectors // block):
            piece = p_ref[part, :, pl.ds(chunk * block * SPIN, block * SPIN)]
            apart = dot(piece, table, 1, 1).astype(BF16)
            for spin in range(SPIN):
                o_ref[
                    pl.ds(spin * columns, columns),
                    pl.ds(part * vectors + chunk * block, block),
                ] = apart[:, spin * block : (spin + 1) * block]


def last_kernel(places_ref, m_ref, p_ref, s_ref, *rest):
    o_ref = rest[-1]
    columns = o_ref.shape[2]
    vectors = m_ref.shape[1]
    block = s_ref.shape[0] // SPIN
    packed = m_ref[...].astype(F32)
    turned = jnp.transpose(packed)
    real = (0.5 * (turned - packed)).astype(BF16)
    imag = (0.5 * (packed + turned)).astype(BF16)
    minus = -imag
    right = jnp.concatenate(
        [jnp.concatenate([real, imag], axis=1), jnp.concatenate([minus, real], axis=1)], axis=0
    )
    product = dot(p_ref[...], right, 1, 0).astype(BF16)
    for part in range(2):
        for chunk in range(vectors // block):
            at = part * vectors + chunk * block
            piece = jnp.concatenate(
                [product[spin * columns : (spin + 1) * columns, at : at + block] for spin in range(SPIN)],
                axis=1,
            )
            o_ref[0, part, :, pl.ds(chunk * block * SPIN, block * SPIN)] = dot(
                piece, s_ref[...], 1, 0
            ).astype(BF16)


def last_call(places, packed, spins, table, shape, result=None):
    vectors = packed.shape[1]
    count = packed.shape[0] // vectors
    specs = [
        pl.BlockSpec((vectors, vectors), lambda i, at: (i, 0)),
        pl.BlockSpec(spins.shape, lambda i, at: (0, 0)),
        pl.BlockSpec(table.shape, lambda i, at: (0, 0)),
    ]
    args = [places, packed, spins, table]
    aliases = {}
    if result is not None:
        specs.append(pl.BlockSpec(memory_space=pl.ANY))
        args.append(result)
        aliases = {4: 0}
    return pl.pallas_call(
        last_kernel,
        grid_spec=pltpu.PrefetchScalarGridSpec(
            num_scalar_prefetch=1,
            grid=(count,),
            in_specs=specs,
            out_specs=pl.BlockSpec((1,) + shape[1:], lambda i, at: (at[i], 0, 0, 0)),
        ),
        out_shape=jax.ShapeDtypeStruct(shape, BF16),
        input_output_aliases=aliases,
        cost_estimate=pl.CostEstimate(flops=count * 800_000_000, bytes_accessed=count * 1_000_000, transcendentals=0),
    )(*args)


def sum_over_space(partial, ranks):
    rows, width = partial.shape
    pieces = lax.all_to_all(
        partial.reshape(ranks, rows // ranks, width), "space", 0, 0, tiled=True
    )
    total = jnp.sum(pieces.astype(F32), axis=0).astype(BF16)
    whole = lax.all_to_all(
        jnp.broadcast_to(total[None], (ranks,) + total.shape), "space", 0, 0, tiled=True
    )
    return whole.reshape(rows, width)


def on_device(eigvecs, links, dirs, peram):
    ranks = lax.axis_size("space")
    vectors, sites = eigvecs.shape[2], eigvecs.shape[4]
    assert sites == LX * LZ and ranks % 2 == 0
    field = jnp.transpose(eigvecs[0], (0, 2, 3, 1)).reshape(6 * sites, vectors)
    link_rows = links[0].reshape(54, sites)
    half = half_rows(sites)
    rows = 6 * half + padded(18)

    payload = jax.ShapeDtypeStruct((rows, vectors), BF16)
    across, along = pl.pallas_call(
        functools.partial(prepare_kernel, sites),
        out_shape=(payload, payload),
        in_specs=[VMEM] * 2,
        out_specs=(VMEM, VMEM),
    )(field, link_rows[18:36])
    from_across = lax.ppermute(across, "space", [(i, i ^ 1) for i in range(ranks)])
    from_along = lax.ppermute(
        along,
        "space",
        [((i + 2) % ranks if i % 2 == 0 else (i - 2) % ranks, i) for i in range(ranks)],
    )
    partner = lax.ppermute(peram[0], "tm", [((i + 1) % 2, i) for i in range(2)])

    flat = pl.pallas_call(
        functools.partial(front_kernel, sites),
        out_shape=jax.ShapeDtypeStruct((2 * vectors, vectors), BF16),
        in_specs=[VMEM] * 2,
        out_specs=VMEM,
        scratch_shapes=[pltpu.VMEM((2, 6 * sites, vectors), F32)],
        cost_estimate=pl.CostEstimate(flops=700_000_000, bytes_accessed=8_000_000, transcendentals=0),
    )(field, jnp.concatenate([link_rows[:18], link_rows[36:]]))
    columns = partner.shape[1]
    spins, table = pl.pallas_call(
        spins_kernel,
        out_shape=(
            jax.ShapeDtypeStruct((SPIN * columns, 2 * vectors), BF16),
            jax.ShapeDtypeStruct((SPIN * 128, SPIN * 128), BF16),
        ),
        in_specs=[VMEM],
        out_specs=(VMEM, VMEM),
        cost_estimate=pl.CostEstimate(flops=500_000_000, bytes_accessed=2_000_000, transcendentals=0),
    )(partner)
    whole_flat = sum_over_space(flat, ranks)
    upright = pl.pallas_call(
        functools.partial(middle_kernel, half),
        out_shape=jax.ShapeDtypeStruct((vectors, vectors), BF16),
        in_specs=[VMEM] * 3,
        out_specs=VMEM,
        scratch_shapes=[pltpu.VMEM((2, 6 * half, vectors), F32)],
        cost_estimate=pl.CostEstimate(flops=400_000_000, bytes_accessed=4_000_000, transcendentals=0),
    )(along, from_across, from_along)
    whole_upright = sum_over_space(upright, ranks)

    count = dirs.shape[0]
    order = jnp.arange(count, dtype=jnp.int32)
    places = jnp.sum(jnp.where(dirs[None, :] == order[:, None], order[None, :], 0), axis=1)
    shape = (count, 2, columns, SPIN * vectors)
    result = last_call(jnp.stack([places[0], places[2]]), whole_flat, spins, table, shape)
    result = last_call(places[1:2], whole_upright, spins, table, shape, result)
    return result[None]


def solution(mesh):
    placed = (
        P(("parts", "tm"), None, None, None, "space"),
        P(("parts", "tm"), None, None, None, None, "space"),
        P(),
        P(("parts", "tm"), None, "space", None),
    )
    return jax.shard_map(
        on_device,
        mesh=mesh,
        in_specs=placed,
        out_specs=P(("parts", "tm"), None, None, "space", None),
        check_vma=False,
    )
```

```python
import functools

import jax
import jax.numpy as jnp
from jax import lax
from jax.experimental import pallas as pl
from jax.experimental.pallas import tpu as pltpu
from jax.sharding import PartitionSpec as P


SPIN = 4
LX = 9
LZ = 24
F32 = jnp.float32
BF16 = jnp.bfloat16
VMEM = pl.BlockSpec(memory_space=pltpu.VMEM)
ANY = pl.BlockSpec(memory_space=pl.ANY)
PARAMS = pltpu.CompilerParams(vmem_limit_bytes=12 * 1024 * 1024)


def half_rows(sites):
    return 8 * ((sites + 15) // 16)


def padded(count):
    return 8 * ((count + 7) // 8)


def identity(size):
    rows = lax.broadcasted_iota(jnp.int32, (size, size), 0)
    cols = lax.broadcasted_iota(jnp.int32, (size, size), 1)
    return jnp.where(rows == cols, 1.0, 0.0).astype(BF16)


def dot(left, right, left_dim, right_dim):
    return lax.dot_general(
        left, right, (((left_dim,), (right_dim,)), ((), ())), preferred_element_type=F32
    )


def adjoint_product(columns, base, vec):
    real_rows, imag_rows = [], []
    for out in range(3):
        real_sum = imag_sum = None
        for inner in range(3):
            at = base + (inner * 3 + out) * 2
            link_real = columns[:, at : at + 1]
            link_imag = columns[:, at + 1 : at + 2]
            real = link_real * vec[inner] + link_imag * vec[3 + inner]
            imag = link_real * vec[3 + inner] - link_imag * vec[inner]
            real_sum = real if real_sum is None else real_sum + real
            imag_sum = imag if imag_sum is None else imag_sum + imag
        real_rows.append(real_sum)
        imag_rows.append(imag_sum)
    return real_rows + imag_rows


def packed_elemental(w_real, w_imag, v_real, v_imag):
    real = dot(w_real, v_real, 0, 0) + dot(w_imag, v_imag, 0, 0)
    imag = dot(w_real, v_imag, 0, 0) - dot(w_imag, v_real, 0, 0)
    return (real + imag) + jnp.transpose(imag - real)


def prepare_kernel(sites, v_ref, u_ref, across_ref, along_ref):
    half = half_rows(sites)
    overlap = 2 * half - sites
    vectors = v_ref.shape[1]
    parity = lax.rem(lax.axis_index("space"), 2)
    entries = 18

    def fill(ref, upper):
        first = sites - half if upper else 0
        for comp in range(6):
            ref[pl.ds(comp * half, half), :] = v_ref[pl.ds(comp * sites + first, half), :]
        links = u_ref[18:36, first : first + half].astype(F32)
        if upper and overlap:
            lane = lax.broadcasted_iota(jnp.int32, links.shape, 1)
            links = jnp.where(lane < overlap, 0.0, links)
        rows = ref.shape[0] - 6 * half
        block = jnp.concatenate(
            [
                jnp.concatenate([links, jnp.zeros((rows - entries, half), F32)], axis=0),
                jnp.zeros((rows, vectors - half), F32),
            ],
            axis=1,
        )
        ref[pl.ds(6 * half, rows), :] = block.astype(BF16)

    @pl.when(parity == 0)
    def _():
        fill(across_ref, True)
        fill(along_ref, False)

    @pl.when(parity == 1)
    def _():
        fill(across_ref, False)
        fill(along_ref, True)


def front_kernel(sites, v_ref, u_ref, o_ref, w_ref):
    planes = sites // LZ
    vectors = v_ref.shape[1]
    columns = dot(identity(sites), u_ref[...], 1, 1)
    for plane in range(planes):
        slab, along = plane // LX, plane % LX
        start = plane * LZ
        vec = [v_ref[pl.ds(comp * sites + start, LZ), :].astype(F32) for comp in range(6)]
        here = columns[start : start + LZ, :]
        ahead = (slab * LX + (along + 1) % LX) * LZ
        for comp, value in enumerate(adjoint_product(here, 0, vec)):
            w_ref[0, pl.ds(comp * sites + ahead, LZ), :] = value
        for comp, value in enumerate(adjoint_product(here, 36, vec)):
            w_ref[1, pl.ds(comp * sites + start, LZ), :] = pltpu.roll(value, 1, 0)
    real = pl.ds(0, 3 * sites)
    imag = pl.ds(3 * sites, 3 * sites)
    for index in range(2):
        packed = packed_elemental(
            w_ref[index, real, :].astype(BF16),
            w_ref[index, imag, :].astype(BF16),
            v_ref[real, :],
            v_ref[imag, :],
        )
        o_ref[pl.ds(index * vectors, vectors), :] = packed.astype(BF16)


def middle_kernel(half, own_ref, across_ref, along_ref, flat_ref, o_ref, w_ref, pack_ref, sem):
    even = lax.rem(lax.axis_index("space"), 2) == 0
    first = jnp.where(even, own_ref[...], along_ref[...])
    last = jnp.where(even, along_ref[...], own_ref[...])
    middle = across_ref[...]
    ident = identity(half)
    for index, field in enumerate((first, middle)):
        columns = dot(ident, field[6 * half :, :half], 1, 1)
        vec = [field[comp * half : (comp + 1) * half, :].astype(F32) for comp in range(6)]
        for comp, value in enumerate(adjoint_product(columns, 0, vec)):
            part, inner = comp // 3, comp % 3
            w_ref[part, pl.ds((index * 3 + inner) * half, half), :] = value
    v_real = jnp.concatenate([middle[: 3 * half], last[: 3 * half]], axis=0)
    v_imag = jnp.concatenate([middle[3 * half : 6 * half], last[3 * half : 6 * half]], axis=0)
    packed = packed_elemental(w_ref[0].astype(BF16), w_ref[1].astype(BF16), v_real, v_imag)
    del flat_ref
    pack_ref[...] = packed.astype(BF16)
    vectors = packed.shape[0]
    copy = pltpu.make_async_copy(pack_ref, o_ref.at[pl.ds(2 * vectors, vectors)], sem)
    copy.start()
    copy.wait()


def spread(size):
    rows = lax.broadcasted_iota(jnp.int32, (SPIN * size, SPIN * size), 0)
    cols = lax.broadcasted_iota(jnp.int32, (SPIN * size, SPIN * size), 1)
    target = (rows % size) * SPIN + rows // size
    return jnp.where(cols == target, 1.0, 0.0).astype(BF16)


def spins_kernel(p_ref, o_ref, s_ref):
    columns, wide = p_ref.shape[1], p_ref.shape[2]
    vectors = wide // SPIN
    block = 128
    table = spread(block)
    s_ref[...] = table
    for part in range(2):
        for chunk in range(vectors // block):
            piece = p_ref[part, :, pl.ds(chunk * block * SPIN, block * SPIN)]
            apart = dot(piece, table, 1, 1).astype(BF16)
            for spin in range(SPIN):
                o_ref[
                    pl.ds(spin * columns, columns),
                    pl.ds(part * vectors + chunk * block, block),
                ] = apart[:, spin * block : (spin + 1) * block]


def last_kernel(places_ref, m_ref, p_ref, s_ref, *rest):
    o_ref = rest[-1]
    columns = o_ref.shape[2]
    vectors = m_ref.shape[1]
    block = s_ref.shape[0] // SPIN
    packed = m_ref[...].astype(F32)
    turned = jnp.transpose(packed)
    real = (0.5 * (turned - packed)).astype(BF16)
    imag = (0.5 * (packed + turned)).astype(BF16)
    minus = -imag
    right = jnp.concatenate(
        [jnp.concatenate([real, imag], axis=1), jnp.concatenate([minus, real], axis=1)], axis=0
    )
    product = dot(p_ref[...], right, 1, 0).astype(BF16)
    for part in range(2):
        for chunk in range(vectors // block):
            at = part * vectors + chunk * block
            piece = jnp.concatenate(
                [product[spin * columns : (spin + 1) * columns, at : at + block] for spin in range(SPIN)],
                axis=1,
            )
            o_ref[0, part, :, pl.ds(chunk * block * SPIN, block * SPIN)] = dot(
                piece, s_ref[...], 1, 0
            ).astype(BF16)


def last_call(dirs, packed, spins, table, shape):
    vectors = packed.shape[1]

    def place(direction, dirs_ref):
        at = jnp.where(dirs_ref[1] == direction, 1, jnp.where(dirs_ref[2] == direction, 2, 0))
        return at, 0, 0, 0

    return pl.pallas_call(
        last_kernel,
        grid_spec=pltpu.PrefetchScalarGridSpec(
            num_scalar_prefetch=1,
            grid=(shape[0],),
            in_specs=[
                pl.BlockSpec((vectors, vectors), lambda i, at: (lax.rem(2 * i, 3), 0)),
                VMEM,
                VMEM,
            ],
            out_specs=pl.BlockSpec((1,) + shape[1:], place),
        ),
        out_shape=jax.ShapeDtypeStruct(shape, BF16),
        cost_estimate=pl.CostEstimate(
            flops=2_400_000_000, bytes_accessed=3_000_000, transcendentals=0
        ),
        compiler_params=PARAMS,
    )(dirs, packed, spins, table)


def sum_over_space(partial, ranks):
    rows, width = partial.shape
    pieces = lax.all_to_all(partial.reshape(ranks, rows // ranks, width), "space", 0, 0, tiled=True)
    total = jnp.sum(pieces.astype(F32), axis=0).astype(BF16)
    spread_out = jnp.broadcast_to(total[None], (ranks,) + total.shape)
    whole = lax.all_to_all(spread_out, "space", 0, 0, tiled=True)
    return whole.reshape(rows, width)


def blocks(eigvecs, links, dirs, peram):
    ranks = lax.axis_size("space")
    vectors, sites = eigvecs.shape[2], eigvecs.shape[4]
    assert sites == LX * LZ and ranks % 2 == 0
    field = jnp.transpose(eigvecs[0], (0, 2, 3, 1)).reshape(6 * sites, vectors)
    link_rows = links[0].reshape(54, sites)
    half = half_rows(sites)
    rows = 6 * half + padded(18)

    payload = jax.ShapeDtypeStruct((rows, vectors), BF16)
    across, along = pl.pallas_call(
        functools.partial(prepare_kernel, sites),
        out_shape=(payload, payload),
        in_specs=[VMEM] * 2,
        out_specs=(VMEM, VMEM),
        compiler_params=PARAMS,
    )(field, link_rows)
    from_across = lax.ppermute(across, "space", [(i, i ^ 1) for i in range(ranks)])
    from_along = lax.ppermute(
        along,
        "space",
        [((i + 2) % ranks if i % 2 == 0 else (i - 2) % ranks, i) for i in range(ranks)],
    )
    partner = lax.ppermute(peram[0], "tm", [((i + 1) % 2, i) for i in range(2)])

    packed = pl.pallas_call(
        functools.partial(front_kernel, sites),
        out_shape=jax.ShapeDtypeStruct((3 * vectors, vectors), BF16),
        in_specs=[VMEM] * 2,
        out_specs=VMEM,
        scratch_shapes=[pltpu.VMEM((2, 6 * sites, vectors), F32)],
        cost_estimate=pl.CostEstimate(flops=700_000_000, bytes_accessed=8_000_000, transcendentals=0),
        compiler_params=PARAMS,
    )(field, link_rows)
    columns = partner.shape[1]
    spins, table = pl.pallas_call(
        spins_kernel,
        out_shape=(
            jax.ShapeDtypeStruct((SPIN * columns, 2 * vectors), BF16),
            jax.ShapeDtypeStruct((SPIN * 128, SPIN * 128), BF16),
        ),
        in_specs=[VMEM],
        out_specs=(VMEM, VMEM),
        cost_estimate=pl.CostEstimate(flops=500_000_000, bytes_accessed=2_000_000, transcendentals=0),
        compiler_params=PARAMS,
    )(partner)
    packed = pl.pallas_call(
        functools.partial(middle_kernel, half),
        out_shape=jax.ShapeDtypeStruct((3 * vectors, vectors), BF16),
        in_specs=[VMEM] * 3 + [ANY],
        out_specs=ANY,
        scratch_shapes=[
            pltpu.VMEM((2, 6 * half, vectors), F32),
            pltpu.VMEM((vectors, vectors), BF16),
            pltpu.SemaphoreType.DMA,
        ],
        input_output_aliases={3: 0},
        cost_estimate=pl.CostEstimate(
            flops=400_000_000, bytes_accessed=4_000_000, transcendentals=0
        ),
        compiler_params=PARAMS,
    )(along, from_across, from_along, packed)
    packed = sum_over_space(packed, ranks)
    shape = (dirs.shape[0], 2, columns, SPIN * vectors)
    result = last_call(dirs, packed, spins, table, shape)
    return result[None]


def solution(mesh):
    placed = (
        P(("parts", "tm"), None, None, None, "space"),
        P(("parts", "tm"), None, None, None, None, "space"),
        P(),
        P(("parts", "tm"), None, "space", None),
    )
    return jax.shard_map(
        blocks,
        mesh=mesh,
        in_specs=placed,
        out_specs=P(("parts", "tm"), None, None, "space", None),
        check_vma=False,
    )
```

```python
import functools

import jax
import jax.numpy as jnp
from jax import lax
from jax.experimental import pallas as pl
from jax.experimental.pallas import tpu as pltpu
from jax.sharding import PartitionSpec as P


SPIN = 4
LX = 9
LZ = 24
F32 = jnp.float32
BF16 = jnp.bfloat16
VMEM = pl.BlockSpec(memory_space=pltpu.VMEM)
ANY = pl.BlockSpec(memory_space=pl.ANY)
HBM = pl.BlockSpec(memory_space=pltpu.HBM)
VMEM_BYTES = 67_043_328
PARAMS = pltpu.CompilerParams(vmem_limit_bytes=12 * 1024 * 1024)


def half_rows(sites):
    return 8 * ((sites + 15) // 16)


def padded(count):
    return 8 * ((count + 7) // 8)


def identity(size):
    rows = lax.broadcasted_iota(jnp.int32, (size, size), 0)
    cols = lax.broadcasted_iota(jnp.int32, (size, size), 1)
    return jnp.where(rows == cols, 1.0, 0.0).astype(BF16)


def dot(left, right, left_dim, right_dim):
    return lax.dot_general(
        left, right, (((left_dim,), (right_dim,)), ((), ())), preferred_element_type=F32
    )


def adjoint_product(columns, base, vec):
    real_rows, imag_rows = [], []
    for out in range(3):
        real_sum = imag_sum = None
        for inner in range(3):
            at = base + (inner * 3 + out) * 2
            link_real = columns[:, at : at + 1]
            link_imag = columns[:, at + 1 : at + 2]
            real = link_real * vec[inner] + link_imag * vec[3 + inner]
            imag = link_real * vec[3 + inner] - link_imag * vec[inner]
            real_sum = real if real_sum is None else real_sum + real
            imag_sum = imag if imag_sum is None else imag_sum + imag
        real_rows.append(real_sum)
        imag_rows.append(imag_sum)
    return real_rows + imag_rows


def packed_elemental(w_real, w_imag, v_real, v_imag):
    real = dot(w_real, v_real, 0, 0) + dot(w_imag, v_imag, 0, 0)
    imag = dot(w_real, v_imag, 0, 0) - dot(w_imag, v_real, 0, 0)
    return (real + imag) + jnp.transpose(imag - real)


def link_table(u_ref, first, last):
    return jnp.concatenate([u_ref[at].astype(F32) for at in range(first, last)], axis=0)


def prepare_kernel(sites, v_ref, u_ref, across_ref, along_ref, link_ref, sems, link_sem):
    half = half_rows(sites)
    overlap = 2 * half - sites
    vectors = v_ref.shape[1]
    parity = lax.rem(lax.axis_index("space"), 2)
    fetch = pltpu.make_async_copy(u_ref.at[pl.ds(9, 9)], link_ref, link_sem)
    fetch.start()
    copies = []
    for slot, (ref, upper) in enumerate(((across_ref, 1 - parity), (along_ref, parity))):
        for comp in range(6):
            first = pl.multiple_of(comp * sites + upper * (sites - half), 8)
            copy = pltpu.make_async_copy(
                v_ref.at[pl.ds(first, half)],
                ref.at[pl.ds(comp * half, half)],
                sems.at[slot, comp],
            )
            copy.start()
            copies.append(copy)
    fetch.wait()
    links = link_table(link_ref, 0, 9)
    rows = across_ref.shape[0] - 6 * half
    lower = links[:, :half]
    upper = links[:, sites - half :]
    lane = lax.broadcasted_iota(jnp.int32, upper.shape, 1)
    upper = jnp.where(lane < overlap, 0.0, upper)
    for ref, wanted in ((across_ref, 1 - parity), (along_ref, parity)):
        block = jnp.where(wanted == 1, upper, lower)
        block = jnp.concatenate([block, jnp.zeros((rows - block.shape[0], half), F32)], axis=0)
        block = jnp.concatenate([block, jnp.zeros((rows, vectors - half), F32)], axis=1)
        ref[pl.ds(6 * half, rows), :] = block.astype(BF16)
    for copy in copies:
        copy.wait()


def front_kernel(sites, v_ref, u_ref, o_ref, w_ref):
    planes = sites // LZ
    vectors = v_ref.shape[1]
    columns = dot(identity(sites), link_table(u_ref, 0, 27).astype(BF16), 1, 1)
    for plane in range(planes):
        slab, along = plane // LX, plane % LX
        start = plane * LZ
        vec = [v_ref[pl.ds(comp * sites + start, LZ), :].astype(F32) for comp in range(6)]
        here = columns[start : start + LZ, :]
        ahead = (slab * LX + (along + 1) % LX) * LZ
        for comp, value in enumerate(adjoint_product(here, 0, vec)):
            w_ref[0, pl.ds(comp * sites + ahead, LZ), :] = value
        for comp, value in enumerate(adjoint_product(here, 36, vec)):
            w_ref[1, pl.ds(comp * sites + start, LZ), :] = pltpu.roll(value, 1, 0)
    real = pl.ds(0, 3 * sites)
    imag = pl.ds(3 * sites, 3 * sites)
    for index in range(2):
        packed = packed_elemental(
            w_ref[index, real, :].astype(BF16),
            w_ref[index, imag, :].astype(BF16),
            v_ref[real, :],
            v_ref[imag, :],
        )
        o_ref[pl.ds(index * vectors, vectors), :] = packed.astype(BF16)


def middle_kernel(half, own_ref, across_ref, along_ref, flat_ref, o_ref, w_ref, pack_ref, sem):
    even = lax.rem(lax.axis_index("space"), 2) == 0
    first = jnp.where(even, own_ref[...], along_ref[...])
    last = jnp.where(even, along_ref[...], own_ref[...])
    middle = across_ref[...]
    ident = identity(half)
    for index, field in enumerate((first, middle)):
        columns = dot(ident, field[6 * half :, :half], 1, 1)
        vec = [field[comp * half : (comp + 1) * half, :].astype(F32) for comp in range(6)]
        for comp, value in enumerate(adjoint_product(columns, 0, vec)):
            part, inner = comp // 3, comp % 3
            w_ref[part, pl.ds((index * 3 + inner) * half, half), :] = value
    v_real = jnp.concatenate([middle[: 3 * half], last[: 3 * half]], axis=0)
    v_imag = jnp.concatenate([middle[3 * half : 6 * half], last[3 * half : 6 * half]], axis=0)
    packed = packed_elemental(w_ref[0].astype(BF16), w_ref[1].astype(BF16), v_real, v_imag)
    del flat_ref
    pack_ref[...] = packed.astype(BF16)
    vectors = packed.shape[0]
    copy = pltpu.make_async_copy(pack_ref, o_ref.at[pl.ds(2 * vectors, vectors)], sem)
    copy.start()
    copy.wait()


def spread(size):
    rows = lax.broadcasted_iota(jnp.int32, (SPIN * size, SPIN * size), 0)
    cols = lax.broadcasted_iota(jnp.int32, (SPIN * size, SPIN * size), 1)
    target = (rows % size) * SPIN + rows // size
    return jnp.where(cols == target, 1.0, 0.0).astype(BF16)


def spins_kernel(p_ref, minus_ref, plus_ref, s_ref):
    columns, wide = p_ref.shape[1], p_ref.shape[2]
    vectors = wide // SPIN
    block = s_ref.shape[0] // SPIN
    table = spread(block)
    s_ref[...] = table
    for chunk in range(vectors // block):
        at = pl.ds(chunk * block * SPIN, block * SPIN)
        real = dot(p_ref[0, :, at], table, 1, 1)
        imag = dot(p_ref[1, :, at], table, 1, 1)
        less = (0.5 * (real - imag)).astype(BF16)
        more = (0.5 * (real + imag)).astype(BF16)
        to = pl.ds(chunk * block, block)
        for spin in range(SPIN):
            lanes = slice(spin * block, (spin + 1) * block)
            rows = pl.ds(2 * spin * columns, columns)
            below = pl.ds((2 * spin + 1) * columns, columns)
            minus_ref[rows, to] = less[:, lanes]
            minus_ref[below, to] = more[:, lanes]
            plus_ref[rows, to] = -more[:, lanes]
            plus_ref[below, to] = less[:, lanes]


def last_kernel(places_ref, m_ref, minus_ref, plus_ref, s_ref, o_ref):
    columns = o_ref.shape[2]
    vectors = m_ref.shape[1]
    block = s_ref.shape[0] // SPIN
    packed = m_ref[...]
    product = (dot(minus_ref[...], packed, 1, 1) + dot(plus_ref[...], packed, 1, 0)).astype(BF16)
    for chunk in range(vectors // block):
        at = chunk * block
        piece = jnp.concatenate(
            [
                product[2 * spin * columns : 2 * (spin + 1) * columns, at : at + block]
                for spin in range(SPIN)
            ],
            axis=1,
        )
        apart = dot(piece, s_ref[...], 1, 0).astype(BF16)
        to = pl.ds(at * SPIN, block * SPIN)
        o_ref[0, 0, :, to] = apart[:columns]
        o_ref[0, 1, :, to] = apart[columns:]


def last_call(dirs, packed, minus, plus, table, shape):
    vectors = packed.shape[1]

    def place(direction, dirs_ref):
        at = jnp.where(dirs_ref[1] == direction, 1, jnp.where(dirs_ref[2] == direction, 2, 0))
        return at, 0, 0, 0

    return pl.pallas_call(
        last_kernel,
        grid_spec=pltpu.PrefetchScalarGridSpec(
            num_scalar_prefetch=1,
            grid=(shape[0],),
            in_specs=[
                pl.BlockSpec((vectors, vectors), lambda i, at: (lax.rem(2 * i, 3), 0)),
                VMEM,
                VMEM,
                VMEM,
            ],
            out_specs=pl.BlockSpec((1,) + shape[1:], place),
        ),
        out_shape=jax.ShapeDtypeStruct(shape, BF16),
        cost_estimate=pl.CostEstimate(
            flops=2_400_000_000, bytes_accessed=3_000_000, transcendentals=0
        ),
        compiler_params=PARAMS,
    )(dirs, packed, minus, plus, table)


def sum_over_space(partial, ranks):
    rows, width = partial.shape
    near = 4 if ranks % 4 == 0 else 2
    groups = [list(range(first, first + near)) for first in range(0, ranks, near)]
    pieces = lax.all_to_all(
        partial.reshape(near, rows // near, width),
        "space",
        0,
        0,
        axis_index_groups=groups,
        tiled=True,
    )
    total = jnp.sum(pieces.astype(F32), axis=0)
    stride = near
    while stride < ranks:
        other = lax.ppermute(total.astype(BF16), "space", [(i, i ^ stride) for i in range(ranks)])
        total = total + other.astype(F32)
        stride *= 2
    whole = jnp.broadcast_to(total.astype(BF16)[None], (near,) + total.shape)
    whole = lax.all_to_all(whole, "space", 0, 0, axis_index_groups=groups, tiled=True)
    return whole.reshape(rows, width)


def blocks(eigvecs, links, dirs, peram):
    ranks = lax.axis_size("space")
    vectors, sites = eigvecs.shape[2], eigvecs.shape[4]
    assert sites == LX * LZ and ranks % 2 == 0
    field = jnp.transpose(eigvecs[0], (0, 2, 3, 1)).reshape(6 * sites, vectors)
    link_rows = links[0].reshape(27, 2, sites)
    half = half_rows(sites)
    rows = 6 * half + padded(18)

    payload = pltpu.VMEM((rows, vectors), BF16)
    across, along = pl.pallas_call(
        functools.partial(prepare_kernel, sites),
        out_shape=(payload, payload),
        in_specs=[HBM, HBM],
        out_specs=(VMEM, VMEM),
        scratch_shapes=[
            pltpu.VMEM((9, 2, sites), BF16),
            pltpu.SemaphoreType.DMA((2, 6)),
            pltpu.SemaphoreType.DMA,
        ],
        compiler_params=pltpu.CompilerParams(vmem_limit_bytes=VMEM_BYTES - 4 * rows * vectors),
    )(field, link_rows)
    from_across = lax.ppermute(across, "space", [(i, i ^ 1) for i in range(ranks)])
    from_along = lax.ppermute(
        along,
        "space",
        [((i + 2) % ranks if i % 2 == 0 else (i - 2) % ranks, i) for i in range(ranks)],
    )
    partner = lax.ppermute(peram[0], "tm", [((i + 1) % 2, i) for i in range(2)])

    packed = pl.pallas_call(
        functools.partial(front_kernel, sites),
        out_shape=jax.ShapeDtypeStruct((3 * vectors, vectors), BF16),
        in_specs=[VMEM] * 2,
        out_specs=VMEM,
        scratch_shapes=[pltpu.VMEM((2, 6 * sites, vectors), F32)],
        cost_estimate=pl.CostEstimate(flops=700_000_000, bytes_accessed=8_000_000, transcendentals=0),
        compiler_params=PARAMS,
    )(field, link_rows)
    columns = partner.shape[1]
    minus, plus, table = pl.pallas_call(
        spins_kernel,
        out_shape=(
            jax.ShapeDtypeStruct((2 * SPIN * columns, vectors), BF16),
            jax.ShapeDtypeStruct((2 * SPIN * columns, vectors), BF16),
            jax.ShapeDtypeStruct((SPIN * 128, SPIN * 128), BF16),
        ),
        in_specs=[VMEM],
        out_specs=(VMEM, VMEM, VMEM),
        cost_estimate=pl.CostEstimate(flops=500_000_000, bytes_accessed=2_000_000, transcendentals=0),
        compiler_params=PARAMS,
    )(partner)
    packed = pl.pallas_call(
        functools.partial(middle_kernel, half),
        out_shape=jax.ShapeDtypeStruct((3 * vectors, vectors), BF16),
        in_specs=[VMEM] * 3 + [ANY],
        out_specs=ANY,
        scratch_shapes=[
            pltpu.VMEM((2, 6 * half, vectors), F32),
            pltpu.VMEM((vectors, vectors), BF16),
            pltpu.SemaphoreType.DMA,
        ],
        input_output_aliases={3: 0},
        cost_estimate=pl.CostEstimate(
            flops=400_000_000, bytes_accessed=4_000_000, transcendentals=0
        ),
        compiler_params=PARAMS,
    )(along, from_across, from_along, packed)
    packed = sum_over_space(packed, ranks)
    shape = (dirs.shape[0], 2, columns, SPIN * vectors)
    result = last_call(dirs, packed, minus, plus, table, shape)
    return result[None]


def solution(mesh):
    placed = (
        P(("parts", "tm"), None, None, None, "space"),
        P(("parts", "tm"), None, None, None, None, "space"),
        P(),
        P(("parts", "tm"), None, "space", None),
    )
    return jax.shard_map(
        blocks,
        mesh=mesh,
        in_specs=placed,
        out_specs=P(("parts", "tm"), None, None, "space", None),
        check_vma=False,
    )
```

```python
import functools

import jax
import jax.numpy as jnp
from jax import lax
from jax.experimental import pallas as pl
from jax.experimental.pallas import tpu as pltpu
from jax.sharding import PartitionSpec as P


SPIN = 4
LX = 9
LZ = 24
F32 = jnp.float32
BF16 = jnp.bfloat16
VMEM = pl.BlockSpec(memory_space=pltpu.VMEM)
ANY = pl.BlockSpec(memory_space=pl.ANY)
HBM = pl.BlockSpec(memory_space=pltpu.HBM)
VMEM_BYTES = 67_043_328
PARAMS = pltpu.CompilerParams(vmem_limit_bytes=12 * 1024 * 1024)


def half_rows(sites):
    return 8 * ((sites + 15) // 16)


def padded(count):
    return 8 * ((count + 7) // 8)


def identity(size):
    rows = lax.broadcasted_iota(jnp.int32, (size, size), 0)
    cols = lax.broadcasted_iota(jnp.int32, (size, size), 1)
    return jnp.where(rows == cols, 1.0, 0.0).astype(BF16)


def dot(left, right, left_dim, right_dim):
    return lax.dot_general(
        left, right, (((left_dim,), (right_dim,)), ((), ())), preferred_element_type=F32
    )


def adjoint_product(columns, base, vec):
    real_rows, imag_rows = [], []
    for out in range(3):
        real_sum = imag_sum = None
        for inner in range(3):
            at = base + (inner * 3 + out) * 2
            link_real = columns[:, at : at + 1]
            link_imag = columns[:, at + 1 : at + 2]
            real = link_real * vec[inner] + link_imag * vec[3 + inner]
            imag = link_real * vec[3 + inner] - link_imag * vec[inner]
            real_sum = real if real_sum is None else real_sum + real
            imag_sum = imag if imag_sum is None else imag_sum + imag
        real_rows.append(real_sum)
        imag_rows.append(imag_sum)
    return real_rows + imag_rows


def packed_elemental(w_real, w_imag, v_real, v_imag):
    real = dot(w_real, v_real, 0, 0) + dot(w_imag, v_imag, 0, 0)
    imag = dot(w_real, v_imag, 0, 0) - dot(w_imag, v_real, 0, 0)
    return (real + imag) + jnp.transpose(imag - real)


def link_table(u_ref, first, last):
    return jnp.concatenate([u_ref[at].astype(F32) for at in range(first, last)], axis=0)


def prepare_kernel(sites, v_ref, u_ref, across_ref, along_ref, link_ref, sems, link_sem):
    half = half_rows(sites)
    overlap = 2 * half - sites
    vectors = v_ref.shape[1]
    parity = lax.rem(lax.axis_index("space"), 2)
    fetch = pltpu.make_async_copy(u_ref.at[pl.ds(9, 9)], link_ref, link_sem)
    fetch.start()
    copies = []
    for slot, (ref, upper) in enumerate(((across_ref, 1 - parity), (along_ref, parity))):
        for comp in range(6):
            first = pl.multiple_of(comp * sites + upper * (sites - half), 8)
            copy = pltpu.make_async_copy(
                v_ref.at[pl.ds(first, half)],
                ref.at[pl.ds(comp * half, half)],
                sems.at[slot, comp],
            )
            copy.start()
            copies.append(copy)
    fetch.wait()
    links = link_table(link_ref, 0, 9)
    rows = across_ref.shape[0] - 6 * half
    lower = links[:, :half]
    upper = links[:, sites - half :]
    lane = lax.broadcasted_iota(jnp.int32, upper.shape, 1)
    upper = jnp.where(lane < overlap, 0.0, upper)
    for ref, wanted in ((across_ref, 1 - parity), (along_ref, parity)):
        block = jnp.where(wanted == 1, upper, lower)
        block = jnp.concatenate([block, jnp.zeros((rows - block.shape[0], half), F32)], axis=0)
        block = jnp.concatenate([block, jnp.zeros((rows, vectors - half), F32)], axis=1)
        ref[pl.ds(6 * half, rows), :] = block.astype(BF16)
    for copy in copies:
        copy.wait()


def front_kernel(sites, v_ref, u_ref, o_ref, w_ref):
    planes = sites // LZ
    vectors = v_ref.shape[1]
    columns = dot(identity(sites), link_table(u_ref, 0, 27).astype(BF16), 1, 1)
    for plane in range(planes):
        slab, along = plane // LX, plane % LX
        start = plane * LZ
        vec = [v_ref[pl.ds(comp * sites + start, LZ), :].astype(F32) for comp in range(6)]
        here = columns[start : start + LZ, :]
        ahead = (slab * LX + (along + 1) % LX) * LZ
        for comp, value in enumerate(adjoint_product(here, 0, vec)):
            w_ref[0, pl.ds(comp * sites + ahead, LZ), :] = value
        for comp, value in enumerate(adjoint_product(here, 36, vec)):
            w_ref[1, pl.ds(comp * sites + start, LZ), :] = pltpu.roll(value, 1, 0)
    real = pl.ds(0, 3 * sites)
    imag = pl.ds(3 * sites, 3 * sites)
    for index in range(2):
        packed = packed_elemental(
            w_ref[index, real, :].astype(BF16),
            w_ref[index, imag, :].astype(BF16),
            v_ref[real, :],
            v_ref[imag, :],
        )
        o_ref[pl.ds(index * vectors, vectors), :] = packed.astype(BF16)


def pair_product(half, left_ref, right_ref, w_ref):
    even = lax.rem(lax.axis_index("space"), 2) == 0
    left, right = left_ref[...], right_ref[...]
    field = jnp.where(even, left, right)
    ahead = jnp.where(even, right, left)
    columns = dot(identity(half), field[6 * half :, :half], 1, 1)
    vec = [field[comp * half : (comp + 1) * half, :].astype(F32) for comp in range(6)]
    for comp, value in enumerate(adjoint_product(columns, 0, vec)):
        w_ref[pl.ds(comp * half, half), :] = value
    return packed_elemental(
        w_ref[pl.ds(0, 3 * half), :].astype(BF16),
        w_ref[pl.ds(3 * half, 3 * half), :].astype(BF16),
        ahead[: 3 * half],
        ahead[3 * half : 6 * half],
    )


def first_pair_kernel(half, own_ref, across_ref, o_ref, w_ref):
    o_ref[...] = pair_product(half, own_ref, across_ref, w_ref)


def second_pair_kernel(half, across_ref, along_ref, flat_ref, first_ref, o_ref, w_ref):
    done = flat_ref.shape[0]
    o_ref[pl.ds(0, done), :] = flat_ref[...]
    packed = first_ref[...] + pair_product(half, across_ref, along_ref, w_ref)
    o_ref[pl.ds(done, packed.shape[0]), :] = packed.astype(BF16)


def spread(size):
    rows = lax.broadcasted_iota(jnp.int32, (SPIN * size, SPIN * size), 0)
    cols = lax.broadcasted_iota(jnp.int32, (SPIN * size, SPIN * size), 1)
    target = (rows % size) * SPIN + rows // size
    return jnp.where(cols == target, 1.0, 0.0).astype(BF16)


def spins_kernel(p_ref, minus_ref, plus_ref, s_ref):
    columns, wide = p_ref.shape[1], p_ref.shape[2]
    vectors = wide // SPIN
    block = s_ref.shape[0] // SPIN
    table = spread(block)
    s_ref[...] = table
    for chunk in range(vectors // block):
        at = pl.ds(chunk * block * SPIN, block * SPIN)
        real = dot(p_ref[0, :, at], table, 1, 1)
        imag = dot(p_ref[1, :, at], table, 1, 1)
        less = (0.5 * (real - imag)).astype(BF16)
        more = (0.5 * (real + imag)).astype(BF16)
        to = pl.ds(chunk * block, block)
        for spin in range(SPIN):
            lanes = slice(spin * block, (spin + 1) * block)
            rows = pl.ds(2 * spin * columns, columns)
            below = pl.ds((2 * spin + 1) * columns, columns)
            minus_ref[rows, to] = less[:, lanes]
            minus_ref[below, to] = more[:, lanes]
            plus_ref[rows, to] = -more[:, lanes]
            plus_ref[below, to] = less[:, lanes]


def last_kernel(dirs_ref, m_ref, minus_ref, plus_ref, s_ref, o_ref, product_ref, whole_ref, sems):
    vectors = m_ref.shape[1]
    columns = o_ref.shape[2]
    block = s_ref.shape[0] // SPIN
    copies = []
    for index, direction in enumerate((0, 2, 1)):
        packed = m_ref[pl.ds(index * vectors, vectors), :]
        for spin in range(SPIN):
            rows = pl.ds(2 * spin * columns, 2 * columns)
            product_ref[index % 2, rows, :] = (
                dot(minus_ref[rows, :], packed, 1, 1) + dot(plus_ref[rows, :], packed, 1, 0)
            ).astype(BF16)
        place = jnp.where(dirs_ref[1] == direction, 1, jnp.where(dirs_ref[2] == direction, 2, 0))
        for chunk in range(vectors // block):
            piece = jnp.concatenate(
                [
                    product_ref[
                        index % 2,
                        pl.ds(2 * spin * columns, 2 * columns),
                        pl.ds(chunk * block, block),
                    ]
                    for spin in range(SPIN)
                ],
                axis=1,
            )
            apart = dot(piece, s_ref[...], 1, 0).astype(BF16)
            to = pl.ds(chunk * block * SPIN, block * SPIN)
            whole_ref[index, 0, :, to] = apart[:columns]
            whole_ref[index, 1, :, to] = apart[columns:]
            copy = pltpu.make_async_copy(
                whole_ref.at[index, :, :, to], o_ref.at[place, :, :, to], sems.at[index, chunk]
            )
            copy.start()
            copies.append(copy)
    for copy in copies:
        copy.wait()


def last_call(dirs, packed, minus, plus, table, shape):
    vectors = packed.shape[1]
    return pl.pallas_call(
        last_kernel,
        in_specs=[pl.BlockSpec(memory_space=pltpu.SMEM)] + [VMEM] * 4,
        out_specs=HBM,
        out_shape=jax.ShapeDtypeStruct(shape, BF16),
        scratch_shapes=[
            pltpu.VMEM((2,) + minus.shape, BF16),
            pltpu.VMEM(shape, BF16),
            pltpu.SemaphoreType.DMA((shape[0], vectors * SPIN // table.shape[0])),
        ],
        cost_estimate=pl.CostEstimate(
            flops=2_400_000_000, bytes_accessed=3_000_000, transcendentals=0
        ),
        compiler_params=PARAMS,
    )(dirs, packed, minus, plus, table)


def sum_over_space(partial, ranks):
    rows, width = partial.shape
    near = 4 if ranks % 4 == 0 else 2
    groups = [list(range(first, first + near)) for first in range(0, ranks, near)]
    pieces = lax.all_to_all(
        partial.reshape(near, rows // near, width),
        "space",
        0,
        0,
        axis_index_groups=groups,
        tiled=True,
    )
    total = jnp.sum(pieces.astype(F32), axis=0)
    stride = near
    while stride < ranks:
        other = lax.ppermute(total.astype(BF16), "space", [(i, i ^ stride) for i in range(ranks)])
        total = total + other.astype(F32)
        stride *= 2
    whole = jnp.broadcast_to(total.astype(BF16)[None], (near,) + total.shape)
    whole = lax.all_to_all(whole, "space", 0, 0, axis_index_groups=groups, tiled=True)
    return whole.reshape(rows, width)


def blocks(eigvecs, links, dirs, peram):
    ranks = lax.axis_size("space")
    vectors, sites = eigvecs.shape[2], eigvecs.shape[4]
    assert sites == LX * LZ and ranks % 2 == 0
    field = jnp.transpose(eigvecs[0], (0, 2, 3, 1)).reshape(6 * sites, vectors)
    link_rows = links[0].reshape(27, 2, sites)
    half = half_rows(sites)
    rows = 6 * half + padded(18)

    payload = pltpu.VMEM((rows, vectors), BF16)
    across, along = pl.pallas_call(
        functools.partial(prepare_kernel, sites),
        out_shape=(payload, payload),
        in_specs=[HBM, HBM],
        out_specs=(VMEM, VMEM),
        scratch_shapes=[
            pltpu.VMEM((9, 2, sites), BF16),
            pltpu.SemaphoreType.DMA((2, 6)),
            pltpu.SemaphoreType.DMA,
        ],
        compiler_params=pltpu.CompilerParams(vmem_limit_bytes=VMEM_BYTES - 4 * rows * vectors),
    )(field, link_rows)
    from_across = lax.ppermute(across, "space", [(i, i ^ 1) for i in range(ranks)])
    from_along = lax.ppermute(
        along,
        "space",
        [((i + 2) % ranks if i % 2 == 0 else (i - 2) % ranks, i) for i in range(ranks)],
    )
    partner = lax.ppermute(peram[0], "tm", [((i + 1) % 2, i) for i in range(2)])

    flat = pl.pallas_call(
        functools.partial(front_kernel, sites),
        out_shape=jax.ShapeDtypeStruct((2 * vectors, vectors), BF16),
        in_specs=[VMEM] * 2,
        out_specs=VMEM,
        scratch_shapes=[pltpu.VMEM((2, 6 * sites, vectors), F32)],
        cost_estimate=pl.CostEstimate(flops=700_000_000, bytes_accessed=8_000_000, transcendentals=0),
        compiler_params=PARAMS,
    )(field, link_rows)
    columns = partner.shape[1]
    minus, plus, table = pl.pallas_call(
        spins_kernel,
        out_shape=(
            jax.ShapeDtypeStruct((2 * SPIN * columns, vectors), BF16),
            jax.ShapeDtypeStruct((2 * SPIN * columns, vectors), BF16),
            jax.ShapeDtypeStruct((SPIN * 128, SPIN * 128), BF16),
        ),
        in_specs=[VMEM],
        out_specs=(VMEM, VMEM, VMEM),
        cost_estimate=pl.CostEstimate(flops=500_000_000, bytes_accessed=2_000_000, transcendentals=0),
        compiler_params=PARAMS,
    )(partner)
    pair_cost = pl.CostEstimate(flops=200_000_000, bytes_accessed=2_000_000, transcendentals=0)
    pair_scratch = [pltpu.VMEM((6 * half, vectors), F32)]
    upright = pl.pallas_call(
        functools.partial(first_pair_kernel, half),
        out_shape=jax.ShapeDtypeStruct((vectors, vectors), F32),
        in_specs=[VMEM] * 2,
        out_specs=VMEM,
        scratch_shapes=pair_scratch,
        cost_estimate=pair_cost,
        compiler_params=PARAMS,
    )(along, from_across)
    packed = pl.pallas_call(
        functools.partial(second_pair_kernel, half),
        out_shape=jax.ShapeDtypeStruct((3 * vectors, vectors), BF16),
        in_specs=[VMEM] * 4,
        out_specs=VMEM,
        scratch_shapes=pair_scratch,
        cost_estimate=pair_cost,
        compiler_params=PARAMS,
    )(from_across, from_along, flat, upright)
    packed = sum_over_space(packed, ranks)
    shape = (dirs.shape[0], 2, columns, SPIN * vectors)
    result = last_call(dirs, packed, minus, plus, table, shape)
    return result[None]


def solution(mesh):
    placed = (
        P(("parts", "tm"), None, None, None, "space"),
        P(("parts", "tm"), None, None, None, None, "space"),
        P(),
        P(("parts", "tm"), None, "space", None),
    )
    return jax.shard_map(
        blocks,
        mesh=mesh,
        in_specs=placed,
        out_specs=P(("parts", "tm"), None, None, "space", None),
        check_vma=False,
    )
```

```python
import functools

import jax
import jax.numpy as jnp
from jax import lax
from jax.experimental import pallas as pl
from jax.experimental.pallas import tpu as pltpu
from jax.sharding import PartitionSpec as P


SPIN = 4
LX = 9
LZ = 24
F32 = jnp.float32
BF16 = jnp.bfloat16
VMEM = pl.BlockSpec(memory_space=pltpu.VMEM)
ANY = pl.BlockSpec(memory_space=pl.ANY)
HBM = pl.BlockSpec(memory_space=pltpu.HBM)
VMEM_BYTES = 67_043_328
PARAMS = pltpu.CompilerParams(vmem_limit_bytes=12 * 1024 * 1024)


def half_rows(sites):
    return 8 * ((sites + 15) // 16)


def padded(count):
    return 8 * ((count + 7) // 8)


def identity(size):
    rows = lax.broadcasted_iota(jnp.int32, (size, size), 0)
    cols = lax.broadcasted_iota(jnp.int32, (size, size), 1)
    return jnp.where(rows == cols, 1.0, 0.0).astype(BF16)


def dot(left, right, left_dim, right_dim):
    return lax.dot_general(
        left, right, (((left_dim,), (right_dim,)), ((), ())), preferred_element_type=F32
    )


def adjoint_product(columns, base, vec):
    real_rows, imag_rows = [], []
    for out in range(3):
        real_sum = imag_sum = None
        for inner in range(3):
            at = base + (inner * 3 + out) * 2
            link_real = columns[:, at : at + 1]
            link_imag = columns[:, at + 1 : at + 2]
            real = link_real * vec[inner] + link_imag * vec[3 + inner]
            imag = link_real * vec[3 + inner] - link_imag * vec[inner]
            real_sum = real if real_sum is None else real_sum + real
            imag_sum = imag if imag_sum is None else imag_sum + imag
        real_rows.append(real_sum)
        imag_rows.append(imag_sum)
    return real_rows + imag_rows


def packed_elemental(w_real, w_imag, v_real, v_imag):
    real = dot(w_real, v_real, 0, 0) + dot(w_imag, v_imag, 0, 0)
    imag = dot(w_real, v_imag, 0, 0) - dot(w_imag, v_real, 0, 0)
    return (real + imag) + jnp.transpose(imag - real)


def link_table(u_ref, first, last):
    return jnp.concatenate([u_ref[at].astype(F32) for at in range(first, last)], axis=0)


def prepare_kernel(sites, v_ref, u_ref, across_ref, along_ref, link_ref, sems, link_sem):
    half = half_rows(sites)
    overlap = 2 * half - sites
    vectors = v_ref.shape[1]
    parity = lax.rem(lax.axis_index("space"), 2)
    fetch = pltpu.make_async_copy(u_ref.at[pl.ds(9, 9)], link_ref, link_sem)
    fetch.start()
    copies = []
    for slot, (ref, upper) in enumerate(((across_ref, 1 - parity), (along_ref, parity))):
        for comp in range(6):
            first = pl.multiple_of(comp * sites + upper * (sites - half), 8)
            copy = pltpu.make_async_copy(
                v_ref.at[pl.ds(first, half)],
                ref.at[pl.ds(comp * half, half)],
                sems.at[slot, comp],
            )
            copy.start()
            copies.append(copy)
    fetch.wait()
    links = link_table(link_ref, 0, 9)
    rows = across_ref.shape[0] - 6 * half
    lower = links[:, :half]
    upper = links[:, sites - half :]
    lane = lax.broadcasted_iota(jnp.int32, upper.shape, 1)
    upper = jnp.where(lane < overlap, 0.0, upper)
    for ref, wanted in ((across_ref, 1 - parity), (along_ref, parity)):
        block = jnp.where(wanted == 1, upper, lower)
        block = jnp.concatenate([block, jnp.zeros((rows - block.shape[0], half), F32)], axis=0)
        block = jnp.concatenate([block, jnp.zeros((rows, vectors - half), F32)], axis=1)
        ref[pl.ds(6 * half, rows), :] = block.astype(BF16)
    for copy in copies:
        copy.wait()


def front_kernel(sites, v_ref, u_ref, o_ref, w_ref):
    planes = sites // LZ
    vectors = v_ref.shape[1]
    columns = dot(identity(sites), link_table(u_ref, 0, 27).astype(BF16), 1, 1)
    for plane in range(planes):
        slab, along = plane // LX, plane % LX
        start = plane * LZ
        vec = [v_ref[pl.ds(comp * sites + start, LZ), :].astype(F32) for comp in range(6)]
        here = columns[start : start + LZ, :]
        ahead = (slab * LX + (along + 1) % LX) * LZ
        for comp, value in enumerate(adjoint_product(here, 0, vec)):
            w_ref[0, pl.ds(comp * sites + ahead, LZ), :] = value
        for comp, value in enumerate(adjoint_product(here, 36, vec)):
            w_ref[1, pl.ds(comp * sites + start, LZ), :] = pltpu.roll(value, 1, 0)
    real = pl.ds(0, 3 * sites)
    imag = pl.ds(3 * sites, 3 * sites)
    for index in range(2):
        packed = packed_elemental(
            w_ref[index, real, :].astype(BF16),
            w_ref[index, imag, :].astype(BF16),
            v_ref[real, :],
            v_ref[imag, :],
        )
        o_ref[pl.ds(index * vectors, vectors), :] = packed.astype(BF16)


def rotated(half, field, w_ref):
    columns = dot(identity(half), field[6 * half :, :half], 1, 1)
    vec = [field[comp * half : (comp + 1) * half, :].astype(F32) for comp in range(6)]
    for comp, value in enumerate(adjoint_product(columns, 0, vec)):
        w_ref[pl.ds(comp * half, half), :] = value.astype(w_ref.dtype)


def early_kernel(half, own_ref, along_ref, w_ref):
    even = lax.rem(lax.axis_index("space"), 2) == 0
    rotated(half, jnp.where(even, own_ref[...], along_ref[...]), w_ref)


def late_kernel(half, early_ref, own_ref, across_ref, along_ref, flat_ref, o_ref, w_ref):
    done = flat_ref.shape[0]
    o_ref[pl.ds(0, done), :] = flat_ref[...]
    even = lax.rem(lax.axis_index("space"), 2) == 0
    rotated(half, across_ref[...], w_ref)
    real, imag = pl.ds(0, 3 * half), pl.ds(3 * half, 3 * half)
    packed = packed_elemental(
        early_ref[real, :], early_ref[imag, :], across_ref[real, :], across_ref[imag, :]
    ) + packed_elemental(
        w_ref[real, :].astype(BF16),
        w_ref[imag, :].astype(BF16),
        jnp.where(even, along_ref[real, :], own_ref[real, :]),
        jnp.where(even, along_ref[imag, :], own_ref[imag, :]),
    )
    o_ref[pl.ds(done, packed.shape[0]), :] = packed.astype(BF16)


def spread(size):
    rows = lax.broadcasted_iota(jnp.int32, (SPIN * size, SPIN * size), 0)
    cols = lax.broadcasted_iota(jnp.int32, (SPIN * size, SPIN * size), 1)
    target = (rows % size) * SPIN + rows // size
    return jnp.where(cols == target, 1.0, 0.0).astype(BF16)


def spins_kernel(p_ref, minus_ref, plus_ref, s_ref):
    columns, wide = p_ref.shape[1], p_ref.shape[2]
    vectors = wide // SPIN
    block = s_ref.shape[0] // SPIN
    table = spread(block)
    s_ref[...] = table
    for chunk in range(vectors // block):
        at = pl.ds(chunk * block * SPIN, block * SPIN)
        real = dot(p_ref[0, :, at], table, 1, 1)
        imag = dot(p_ref[1, :, at], table, 1, 1)
        less = (0.5 * (real - imag)).astype(BF16)
        more = (0.5 * (real + imag)).astype(BF16)
        to = pl.ds(chunk * block, block)
        for spin in range(SPIN):
            lanes = slice(spin * block, (spin + 1) * block)
            rows = pl.ds(2 * spin * columns, columns)
            below = pl.ds((2 * spin + 1) * columns, columns)
            minus_ref[rows, to] = less[:, lanes]
            minus_ref[below, to] = more[:, lanes]
            plus_ref[rows, to] = -more[:, lanes]
            plus_ref[below, to] = less[:, lanes]


def last_kernel(dirs_ref, m_ref, minus_ref, plus_ref, s_ref, o_ref, product_ref, whole_ref, sems):
    vectors = m_ref.shape[1]
    columns = o_ref.shape[2]
    block = s_ref.shape[0] // SPIN
    copies = []
    for index, direction in enumerate((0, 2, 1)):
        packed = m_ref[pl.ds(index * vectors, vectors), :]
        for spin in range(SPIN):
            rows = pl.ds(2 * spin * columns, 2 * columns)
            product_ref[index % 2, rows, :] = (
                dot(minus_ref[rows, :], packed, 1, 1) + dot(plus_ref[rows, :], packed, 1, 0)
            ).astype(BF16)
        place = jnp.where(dirs_ref[1] == direction, 1, jnp.where(dirs_ref[2] == direction, 2, 0))
        for chunk in range(vectors // block):
            piece = jnp.concatenate(
                [
                    product_ref[
                        index % 2,
                        pl.ds(2 * spin * columns, 2 * columns),
                        pl.ds(chunk * block, block),
                    ]
                    for spin in range(SPIN)
                ],
                axis=1,
            )
            apart = dot(piece, s_ref[...], 1, 0).astype(BF16)
            to = pl.ds(chunk * block * SPIN, block * SPIN)
            whole_ref[index, 0, :, to] = apart[:columns]
            whole_ref[index, 1, :, to] = apart[columns:]
            copy = pltpu.make_async_copy(
                whole_ref.at[index, :, :, to], o_ref.at[place, :, :, to], sems.at[index, chunk]
            )
            copy.start()
            copies.append(copy)
    for copy in copies:
        copy.wait()


def last_call(dirs, packed, minus, plus, table, shape):
    vectors = packed.shape[1]
    return pl.pallas_call(
        last_kernel,
        in_specs=[pl.BlockSpec(memory_space=pltpu.SMEM)] + [VMEM] * 4,
        out_specs=HBM,
        out_shape=jax.ShapeDtypeStruct(shape, BF16),
        scratch_shapes=[
            pltpu.VMEM((2,) + minus.shape, BF16),
            pltpu.VMEM(shape, BF16),
            pltpu.SemaphoreType.DMA((shape[0], vectors * SPIN // table.shape[0])),
        ],
        cost_estimate=pl.CostEstimate(
            flops=2_400_000_000, bytes_accessed=3_000_000, transcendentals=0
        ),
        compiler_params=PARAMS,
    )(dirs, packed, minus, plus, table)


def sum_over_space(partial, ranks):
    rows, width = partial.shape
    near = 4 if ranks % 4 == 0 else 2
    groups = [list(range(first, first + near)) for first in range(0, ranks, near)]
    pieces = lax.all_to_all(
        partial.reshape(near, rows // near, width),
        "space",
        0,
        0,
        axis_index_groups=groups,
        tiled=True,
    )
    total = jnp.sum(pieces.astype(F32), axis=0)
    stride = near
    while stride < ranks:
        other = lax.ppermute(total.astype(BF16), "space", [(i, i ^ stride) for i in range(ranks)])
        total = total + other.astype(F32)
        stride *= 2
    whole = jnp.broadcast_to(total.astype(BF16)[None], (near,) + total.shape)
    whole = lax.all_to_all(whole, "space", 0, 0, axis_index_groups=groups, tiled=True)
    return whole.reshape(rows, width)


def blocks(eigvecs, links, dirs, peram):
    ranks = lax.axis_size("space")
    vectors, sites = eigvecs.shape[2], eigvecs.shape[4]
    assert sites == LX * LZ and ranks % 2 == 0
    field = jnp.transpose(eigvecs[0], (0, 2, 3, 1)).reshape(6 * sites, vectors)
    link_rows = links[0].reshape(27, 2, sites)
    half = half_rows(sites)
    rows = 6 * half + padded(18)

    payload = pltpu.VMEM((rows, vectors), BF16)
    across, along = pl.pallas_call(
        functools.partial(prepare_kernel, sites),
        out_shape=(payload, payload),
        in_specs=[HBM, HBM],
        out_specs=(VMEM, VMEM),
        scratch_shapes=[
            pltpu.VMEM((9, 2, sites), BF16),
            pltpu.SemaphoreType.DMA((2, 6)),
            pltpu.SemaphoreType.DMA,
        ],
        compiler_params=pltpu.CompilerParams(vmem_limit_bytes=VMEM_BYTES - 4 * rows * vectors),
    )(field, link_rows)
    from_across = lax.ppermute(across, "space", [(i, i ^ 1) for i in range(ranks)])
    from_along = lax.ppermute(
        along,
        "space",
        [((i + 2) % ranks if i % 2 == 0 else (i - 2) % ranks, i) for i in range(ranks)],
    )
    partner = lax.ppermute(peram[0], "tm", [((i + 1) % 2, i) for i in range(2)])

    flat = pl.pallas_call(
        functools.partial(front_kernel, sites),
        out_shape=jax.ShapeDtypeStruct((2 * vectors, vectors), BF16),
        in_specs=[VMEM] * 2,
        out_specs=VMEM,
        scratch_shapes=[pltpu.VMEM((2, 6 * sites, vectors), F32)],
        cost_estimate=pl.CostEstimate(flops=700_000_000, bytes_accessed=8_000_000, transcendentals=0),
        compiler_params=PARAMS,
    )(field, link_rows)
    columns = partner.shape[1]
    minus, plus, table = pl.pallas_call(
        spins_kernel,
        out_shape=(
            jax.ShapeDtypeStruct((2 * SPIN * columns, vectors), BF16),
            jax.ShapeDtypeStruct((2 * SPIN * columns, vectors), BF16),
            jax.ShapeDtypeStruct((SPIN * 128, SPIN * 128), BF16),
        ),
        in_specs=[VMEM],
        out_specs=(VMEM, VMEM, VMEM),
        cost_estimate=pl.CostEstimate(flops=500_000_000, bytes_accessed=2_000_000, transcendentals=0),
        compiler_params=PARAMS,
    )(partner)
    early = pl.pallas_call(
        functools.partial(early_kernel, half),
        out_shape=jax.ShapeDtypeStruct((6 * half, vectors), BF16),
        in_specs=[VMEM] * 2,
        out_specs=VMEM,
        cost_estimate=pl.CostEstimate(
            flops=20_000_000, bytes_accessed=1_000_000, transcendentals=0
        ),
        compiler_params=PARAMS,
    )(along, from_along)
    packed = pl.pallas_call(
        functools.partial(late_kernel, half),
        out_shape=jax.ShapeDtypeStruct((3 * vectors, vectors), BF16),
        in_specs=[VMEM] * 5,
        out_specs=VMEM,
        scratch_shapes=[pltpu.VMEM((6 * half, vectors), F32)],
        cost_estimate=pl.CostEstimate(
            flops=400_000_000, bytes_accessed=2_000_000, transcendentals=0
        ),
        compiler_params=PARAMS,
    )(early, along, from_across, from_along, flat)
    packed = sum_over_space(packed, ranks)
    shape = (dirs.shape[0], 2, columns, SPIN * vectors)
    result = last_call(dirs, packed, minus, plus, table, shape)
    return result[None]


def solution(mesh):
    placed = (
        P(("parts", "tm"), None, None, None, "space"),
        P(("parts", "tm"), None, None, None, None, "space"),
        P(),
        P(("parts", "tm"), None, "space", None),
    )
    return jax.shard_map(
        blocks,
        mesh=mesh,
        in_specs=placed,
        out_specs=P(("parts", "tm"), None, None, "space", None),
        check_vma=False,
    )
```

```python
import functools

import jax
import jax.numpy as jnp
from jax import lax
from jax.experimental import pallas as pl
from jax.experimental.pallas import tpu as pltpu
from jax.sharding import PartitionSpec as P


SPIN = 4
LX = 9
LZ = 24
F32 = jnp.float32
BF16 = jnp.bfloat16
VMEM = pl.BlockSpec(memory_space=pltpu.VMEM)
ANY = pl.BlockSpec(memory_space=pl.ANY)
HBM = pl.BlockSpec(memory_space=pltpu.HBM)
VMEM_BYTES = 67_043_328
PARAMS = pltpu.CompilerParams(vmem_limit_bytes=12 * 1024 * 1024)


def half_rows(sites):
    return 8 * ((sites + 15) // 16)


def padded(count):
    return 8 * ((count + 7) // 8)


def identity(size):
    rows = lax.broadcasted_iota(jnp.int32, (size, size), 0)
    cols = lax.broadcasted_iota(jnp.int32, (size, size), 1)
    return jnp.where(rows == cols, 1.0, 0.0).astype(BF16)


def dot(left, right, left_dim, right_dim):
    return lax.dot_general(
        left, right, (((left_dim,), (right_dim,)), ((), ())), preferred_element_type=F32
    )


def adjoint_product(columns, base, vec):
    real_rows, imag_rows = [], []
    for out in range(3):
        real_sum = imag_sum = None
        for inner in range(3):
            at = base + (inner * 3 + out) * 2
            link_real = columns[:, at : at + 1]
            link_imag = columns[:, at + 1 : at + 2]
            real = link_real * vec[inner] + link_imag * vec[3 + inner]
            imag = link_real * vec[3 + inner] - link_imag * vec[inner]
            real_sum = real if real_sum is None else real_sum + real
            imag_sum = imag if imag_sum is None else imag_sum + imag
        real_rows.append(real_sum)
        imag_rows.append(imag_sum)
    return real_rows + imag_rows


def packed_elemental(w_real, w_imag, v_real, v_imag):
    real = dot(w_real, v_real, 0, 0) + dot(w_imag, v_imag, 0, 0)
    imag = dot(w_real, v_imag, 0, 0) - dot(w_imag, v_real, 0, 0)
    return (real + imag) + jnp.transpose(imag - real)


def link_table(u_ref, first, last):
    return jnp.concatenate([u_ref[at].astype(F32) for at in range(first, last)], axis=0)


def prepare_kernel(sites, v_ref, u_ref, across_ref, along_ref, link_ref, sems, link_sem):
    half = half_rows(sites)
    overlap = 2 * half - sites
    vectors = v_ref.shape[1]
    parity = lax.rem(lax.axis_index("space"), 2)
    fetch = pltpu.make_async_copy(u_ref.at[pl.ds(9, 9)], link_ref, link_sem)
    fetch.start()
    copies = []
    for slot, (ref, upper) in enumerate(((across_ref, 1 - parity), (along_ref, parity))):
        for comp in range(6):
            first = pl.multiple_of(comp * sites + upper * (sites - half), 8)
            copy = pltpu.make_async_copy(
                v_ref.at[pl.ds(first, half)],
                ref.at[pl.ds(comp * half, half)],
                sems.at[slot, comp],
            )
            copy.start()
            copies.append(copy)
    fetch.wait()
    links = link_table(link_ref, 0, 9)
    rows = across_ref.shape[0] - 6 * half
    lower = links[:, :half]
    upper = links[:, sites - half :]
    lane = lax.broadcasted_iota(jnp.int32, upper.shape, 1)
    upper = jnp.where(lane < overlap, 0.0, upper)
    for ref, wanted in ((across_ref, 1 - parity), (along_ref, parity)):
        block = jnp.where(wanted == 1, upper, lower)
        block = jnp.concatenate([block, jnp.zeros((rows - block.shape[0], half), F32)], axis=0)
        block = jnp.concatenate([block, jnp.zeros((rows, vectors - half), F32)], axis=1)
        ref[pl.ds(6 * half, rows), :] = block.astype(BF16)
    for copy in copies:
        copy.wait()


def front_kernel(sites, v_ref, u_ref, o_ref, w_ref):
    planes = sites // LZ
    vectors = v_ref.shape[1]
    columns = dot(identity(sites), link_table(u_ref, 0, 27).astype(BF16), 1, 1)
    for plane in range(planes):
        slab, along = plane // LX, plane % LX
        start = plane * LZ
        vec = [v_ref[pl.ds(comp * sites + start, LZ), :].astype(F32) for comp in range(6)]
        here = columns[start : start + LZ, :]
        ahead = (slab * LX + (along + 1) % LX) * LZ
        for comp, value in enumerate(adjoint_product(here, 0, vec)):
            w_ref[0, pl.ds(comp * sites + ahead, LZ), :] = value
        for comp, value in enumerate(adjoint_product(here, 36, vec)):
            w_ref[1, pl.ds(comp * sites + start, LZ), :] = pltpu.roll(value, 1, 0)
    real = pl.ds(0, 3 * sites)
    imag = pl.ds(3 * sites, 3 * sites)
    for index in range(2):
        packed = packed_elemental(
            w_ref[index, real, :].astype(BF16),
            w_ref[index, imag, :].astype(BF16),
            v_ref[real, :],
            v_ref[imag, :],
        )
        o_ref[pl.ds(index * vectors, vectors), :] = packed.astype(BF16)


def rotated(half, field, w_ref):
    columns = dot(identity(half), field[6 * half :, :half], 1, 1)
    vec = [field[comp * half : (comp + 1) * half, :].astype(F32) for comp in range(6)]
    for comp, value in enumerate(adjoint_product(columns, 0, vec)):
        w_ref[pl.ds(comp * half, half), :] = value.astype(w_ref.dtype)


def early_kernel(half, own_ref, along_ref, w_ref):
    even = lax.rem(lax.axis_index("space"), 2) == 0
    rotated(half, jnp.where(even, own_ref[...], along_ref[...]), w_ref)


def late_kernel(half, early_ref, own_ref, across_ref, along_ref, flat_ref, *rest):
    chunks, w_ref, y_ref = rest[:-2], rest[-2], rest[-1]
    near = len(chunks)
    even = lax.rem(lax.axis_index("space"), 2) == 0
    rotated(half, across_ref[...], w_ref)
    real, imag = pl.ds(0, 3 * half), pl.ds(3 * half, 3 * half)
    packed = packed_elemental(
        early_ref[real, :], early_ref[imag, :], across_ref[real, :], across_ref[imag, :]
    ) + packed_elemental(
        w_ref[real, :].astype(BF16),
        w_ref[imag, :].astype(BF16),
        jnp.where(even, along_ref[real, :], own_ref[real, :]),
        jnp.where(even, along_ref[imag, :], own_ref[imag, :]),
    )
    y_ref[...] = packed.astype(BF16)
    place = lax.rem(lax.axis_index("space"), near)
    wide, narrow = flat_ref.shape[0] // near, y_ref.shape[0] // near
    for partner, chunk_ref in enumerate(chunks):
        chunk = jnp.bitwise_xor(place, partner)
        chunk_ref[pl.ds(0, wide), :] = flat_ref[pl.ds(pl.multiple_of(chunk * wide, wide), wide), :]
        chunk_ref[pl.ds(wide, narrow), :] = y_ref[
            pl.ds(pl.multiple_of(chunk * narrow, narrow), narrow), :
        ]


def spread(size):
    rows = lax.broadcasted_iota(jnp.int32, (SPIN * size, SPIN * size), 0)
    cols = lax.broadcasted_iota(jnp.int32, (SPIN * size, SPIN * size), 1)
    target = (rows % size) * SPIN + rows // size
    return jnp.where(cols == target, 1.0, 0.0).astype(BF16)


def spins_kernel(p_ref, minus_ref, plus_ref, s_ref):
    columns, wide = p_ref.shape[1], p_ref.shape[2]
    vectors = wide // SPIN
    block = 128
    table = spread(block)
    s_ref[...] = spread(s_ref.shape[0] // SPIN)
    for chunk in range(vectors // block):
        at = pl.ds(chunk * block * SPIN, block * SPIN)
        real = dot(p_ref[0, :, at], table, 1, 1)
        imag = dot(p_ref[1, :, at], table, 1, 1)
        less = (0.5 * (real - imag)).astype(BF16)
        more = (0.5 * (real + imag)).astype(BF16)
        to = pl.ds(chunk * block, block)
        for spin in range(SPIN):
            lanes = slice(spin * block, (spin + 1) * block)
            rows = pl.ds(2 * spin * columns, columns)
            below = pl.ds((2 * spin + 1) * columns, columns)
            minus_ref[rows, to] = less[:, lanes]
            minus_ref[below, to] = more[:, lanes]
            plus_ref[rows, to] = -more[:, lanes]
            plus_ref[below, to] = less[:, lanes]


def last_kernel(near, dirs_ref, *refs):
    chunks = refs[:near]
    minus_ref, plus_ref, s_ref, o_ref, flat_ref, y_ref, product_ref, whole_ref, sems = refs[near:]
    vectors = y_ref.shape[0]
    columns = o_ref.shape[2]
    block = s_ref.shape[0] // SPIN
    place = lax.rem(lax.axis_index("space"), near)
    wide, narrow = 2 * vectors // near, vectors // near
    for partner, chunk_ref in enumerate(chunks):
        chunk = jnp.bitwise_xor(place, partner)
        flat_ref[pl.ds(pl.multiple_of(chunk * wide, wide), wide), :] = chunk_ref[pl.ds(0, wide), :]
        y_ref[pl.ds(pl.multiple_of(chunk * narrow, narrow), narrow), :] = chunk_ref[
            pl.ds(wide, narrow), :
        ]
    copies = []

    def multiply(direction):
        if direction == 1:
            packed = y_ref[...]
        else:
            packed = flat_ref[pl.ds(direction // 2 * vectors, vectors), :]
        step = 4 * columns
        for first in range(0, 2 * SPIN * columns, step):
            rows = pl.ds(first, step)
            product_ref[direction, rows, :] = (
                dot(minus_ref[rows, :], packed, 1, 1) + dot(plus_ref[rows, :], packed, 1, 0)
            ).astype(BF16)

    def store(direction):
        to_place = jnp.where(dirs_ref[1] == direction, 1, jnp.where(dirs_ref[2] == direction, 2, 0))
        for chunk in range(vectors // block):
            piece = jnp.concatenate(
                [
                    product_ref[
                        direction,
                        pl.ds(2 * spin * columns, 2 * columns),
                        pl.ds(chunk * block, block),
                    ]
                    for spin in range(SPIN)
                ],
                axis=1,
            )
            apart = dot(piece, s_ref[...], 1, 0).astype(BF16)
            to = pl.ds(chunk * block * SPIN, block * SPIN)
            whole_ref[direction, 0, :, to] = apart[:columns]
            whole_ref[direction, 1, :, to] = apart[columns:]
            copy = pltpu.make_async_copy(
                whole_ref.at[direction, :, :, to],
                o_ref.at[to_place, :, :, to],
                sems.at[direction, chunk],
            )
            copy.start()
            copies.append(copy)

    multiply(0)
    multiply(2)
    store(0)
    multiply(1)
    store(2)
    store(1)
    for copy in copies:
        copy.wait()


def last_call(dirs, chunks, minus, plus, table, shape):
    near = len(chunks)
    vectors = chunks[0].shape[1]
    return pl.pallas_call(
        functools.partial(last_kernel, near),
        in_specs=[pl.BlockSpec(memory_space=pltpu.SMEM)] + [VMEM] * (near + 3),
        out_specs=HBM,
        out_shape=jax.ShapeDtypeStruct(shape, BF16),
        scratch_shapes=[
            pltpu.VMEM((2 * vectors, vectors), BF16),
            pltpu.VMEM((vectors, vectors), BF16),
            pltpu.VMEM((shape[0],) + minus.shape, BF16),
            pltpu.VMEM(shape, BF16),
            pltpu.SemaphoreType.DMA((shape[0], vectors * SPIN // table.shape[0])),
        ],
        cost_estimate=pl.CostEstimate(
            flops=2_400_000_000, bytes_accessed=3_000_000, transcendentals=0
        ),
        compiler_params=pltpu.CompilerParams(vmem_limit_bytes=12 * 1024 * 1024),
    )(dirs, *chunks, minus, plus, table)


def swap(block, ranks, distance):
    return lax.ppermute(block, "space", [(i, i ^ distance) for i in range(ranks)])


def sum_over_space(chunks, ranks):
    near = len(chunks)
    total = chunks[0].astype(F32)
    for partner in range(near - 1, 0, -1):
        total = total + swap(chunks[partner], ranks, partner).astype(F32)
    stride = near
    while stride < ranks:
        total = total + swap(total.astype(BF16), ranks, stride).astype(F32)
        stride *= 2
    whole = [total.astype(BF16)]
    for partner in range(1, near):
        whole.append(swap(whole[0], ranks, partner))
    return whole


def blocks(eigvecs, links, dirs, peram):
    ranks = lax.axis_size("space")
    vectors, sites = eigvecs.shape[2], eigvecs.shape[4]
    assert sites == LX * LZ and ranks % 2 == 0
    field = jnp.transpose(eigvecs[0], (0, 2, 3, 1)).reshape(6 * sites, vectors)
    link_rows = links[0].reshape(27, 2, sites)
    half = half_rows(sites)
    rows = 6 * half + padded(18)
    near = 4 if ranks % 4 == 0 else 2

    payload = pltpu.VMEM((rows, vectors), BF16)
    across, along = pl.pallas_call(
        functools.partial(prepare_kernel, sites),
        out_shape=(payload, payload),
        in_specs=[HBM, HBM],
        out_specs=(VMEM, VMEM),
        scratch_shapes=[
            pltpu.VMEM((9, 2, sites), BF16),
            pltpu.SemaphoreType.DMA((2, 6)),
            pltpu.SemaphoreType.DMA,
        ],
        compiler_params=pltpu.CompilerParams(vmem_limit_bytes=VMEM_BYTES - 4 * rows * vectors),
    )(field, link_rows)
    from_across = lax.ppermute(across, "space", [(i, i ^ 1) for i in range(ranks)])
    from_along = lax.ppermute(
        along,
        "space",
        [((i + 2) % ranks if i % 2 == 0 else (i - 2) % ranks, i) for i in range(ranks)],
    )
    partner = lax.ppermute(peram[0], "tm", [((i + 1) % 2, i) for i in range(2)])

    flat = pl.pallas_call(
        functools.partial(front_kernel, sites),
        out_shape=jax.ShapeDtypeStruct((2 * vectors, vectors), BF16),
        in_specs=[VMEM] * 2,
        out_specs=VMEM,
        scratch_shapes=[pltpu.VMEM((2, 6 * sites, vectors), F32)],
        cost_estimate=pl.CostEstimate(flops=700_000_000, bytes_accessed=8_000_000, transcendentals=0),
        compiler_params=PARAMS,
    )(field, link_rows)
    columns = partner.shape[1]
    minus, plus, table = pl.pallas_call(
        spins_kernel,
        out_shape=(
            jax.ShapeDtypeStruct((2 * SPIN * columns, vectors), BF16),
            jax.ShapeDtypeStruct((2 * SPIN * columns, vectors), BF16),
            jax.ShapeDtypeStruct((SPIN * 64, SPIN * 64), BF16),
        ),
        in_specs=[VMEM],
        out_specs=(VMEM, VMEM, VMEM),
        cost_estimate=pl.CostEstimate(flops=500_000_000, bytes_accessed=2_000_000, transcendentals=0),
        compiler_params=PARAMS,
    )(partner)
    early = pl.pallas_call(
        functools.partial(early_kernel, half),
        out_shape=jax.ShapeDtypeStruct((6 * half, vectors), BF16),
        in_specs=[VMEM] * 2,
        out_specs=VMEM,
        cost_estimate=pl.CostEstimate(
            flops=20_000_000, bytes_accessed=1_000_000, transcendentals=0
        ),
        compiler_params=PARAMS,
    )(along, from_along)
    chunks = pl.pallas_call(
        functools.partial(late_kernel, half),
        out_shape=[jax.ShapeDtypeStruct((3 * vectors // near, vectors), BF16)] * near,
        in_specs=[VMEM] * 5,
        out_specs=[VMEM] * near,
        scratch_shapes=[pltpu.VMEM((6 * half, vectors), F32), pltpu.VMEM((vectors, vectors), BF16)],
        cost_estimate=pl.CostEstimate(
            flops=400_000_000, bytes_accessed=2_000_000, transcendentals=0
        ),
        compiler_params=PARAMS,
    )(early, along, from_across, from_along, flat)
    chunks = sum_over_space(chunks, ranks)
    shape = (dirs.shape[0], 2, columns, SPIN * vectors)
    result = last_call(dirs, chunks, minus, plus, table, shape)
    return result[None]


def solution(mesh):
    placed = (
        P(("parts", "tm"), None, None, None, "space"),
        P(("parts", "tm"), None, None, None, None, "space"),
        P(),
        P(("parts", "tm"), None, "space", None),
    )
    return jax.shard_map(
        blocks,
        mesh=mesh,
        in_specs=placed,
        out_specs=P(("parts", "tm"), None, None, "space", None),
        check_vma=False,
    )
```

```python
import functools

import jax
import jax.numpy as jnp
from jax import lax
from jax.experimental import pallas as pl
from jax.experimental.pallas import tpu as pltpu
from jax.sharding import PartitionSpec as P


SPIN = 4
LX = 9
LZ = 24
F32 = jnp.float32
BF16 = jnp.bfloat16
VMEM = pl.BlockSpec(memory_space=pltpu.VMEM)
ANY = pl.BlockSpec(memory_space=pl.ANY)
HBM = pl.BlockSpec(memory_space=pltpu.HBM)
VMEM_BYTES = 67_043_328
PARAMS = pltpu.CompilerParams(vmem_limit_bytes=12 * 1024 * 1024)


def half_rows(sites):
    return 8 * ((sites + 15) // 16)


def padded(count):
    return 8 * ((count + 7) // 8)


def identity(size):
    rows = lax.broadcasted_iota(jnp.int32, (size, size), 0)
    cols = lax.broadcasted_iota(jnp.int32, (size, size), 1)
    return jnp.where(rows == cols, 1.0, 0.0).astype(BF16)


def dot(left, right, left_dim, right_dim):
    return lax.dot_general(
        left, right, (((left_dim,), (right_dim,)), ((), ())), preferred_element_type=F32
    )


def adjoint_product(columns, base, vec):
    real_rows, imag_rows = [], []
    for out in range(3):
        real_sum = imag_sum = None
        for inner in range(3):
            at = base + (inner * 3 + out) * 2
            link_real = columns[:, at : at + 1]
            link_imag = columns[:, at + 1 : at + 2]
            real = link_real * vec[inner] + link_imag * vec[3 + inner]
            imag = link_real * vec[3 + inner] - link_imag * vec[inner]
            real_sum = real if real_sum is None else real_sum + real
            imag_sum = imag if imag_sum is None else imag_sum + imag
        real_rows.append(real_sum)
        imag_rows.append(imag_sum)
    return real_rows + imag_rows


def packed_elemental(w_real, w_imag, v_real, v_imag):
    real = dot(w_real, v_real, 0, 0) + dot(w_imag, v_imag, 0, 0)
    imag = dot(w_real, v_imag, 0, 0) - dot(w_imag, v_real, 0, 0)
    return (real + imag) + jnp.transpose(imag - real)


def link_table(u_ref, first, last):
    return jnp.concatenate([u_ref[at].astype(F32) for at in range(first, last)], axis=0)


def prepare_kernel(sites, v_ref, u_ref, across_ref, along_ref, link_ref, sems, link_sem):
    half = half_rows(sites)
    overlap = 2 * half - sites
    vectors = v_ref.shape[1]
    parity = lax.rem(lax.axis_index("space"), 2)
    fetch = pltpu.make_async_copy(u_ref.at[pl.ds(9, 9)], link_ref, link_sem)
    fetch.start()
    copies = []
    source = v_ref.reshape(6, sites, vectors)
    for slot, (ref, upper) in enumerate(((along_ref, parity), (across_ref, 1 - parity))):
        first = pl.multiple_of(upper * (sites - half), 8)
        copy = pltpu.make_async_copy(
            source.at[:, pl.ds(first, half)],
            ref.at[pl.ds(0, 6 * half)].reshape(6, half, vectors),
            sems.at[slot, 0],
        )
        copy.start()
        copies.append(copy)
    fetch.wait()
    links = link_table(link_ref, 0, 9)
    rows = across_ref.shape[0] - 6 * half
    lower = links[:, :half]
    upper = links[:, sites - half :]
    lane = lax.broadcasted_iota(jnp.int32, upper.shape, 1)
    upper = jnp.where(lane < overlap, 0.0, upper)
    for ref, wanted in ((across_ref, 1 - parity), (along_ref, parity)):
        block = jnp.where(wanted == 1, upper, lower)
        block = jnp.concatenate([block, jnp.zeros((rows - block.shape[0], half), F32)], axis=0)
        block = jnp.concatenate([block, jnp.zeros((rows, vectors - half), F32)], axis=1)
        ref[pl.ds(6 * half, rows), :] = block.astype(BF16)
    for copy in copies:
        copy.wait()


def front_kernel(sites, v_ref, u_ref, o_ref, w_ref):
    planes = sites // LZ
    vectors = v_ref.shape[1]
    columns = dot(identity(sites), link_table(u_ref, 0, 27).astype(BF16), 1, 1)
    for plane in range(planes):
        slab, along = plane // LX, plane % LX
        start = plane * LZ
        vec = [v_ref[pl.ds(comp * sites + start, LZ), :].astype(F32) for comp in range(6)]
        here = columns[start : start + LZ, :]
        ahead = (slab * LX + (along + 1) % LX) * LZ
        for comp, value in enumerate(adjoint_product(here, 0, vec)):
            w_ref[0, pl.ds(comp * sites + ahead, LZ), :] = value
        for comp, value in enumerate(adjoint_product(here, 36, vec)):
            w_ref[1, pl.ds(comp * sites + start, LZ), :] = pltpu.roll(value, 1, 0)
    real = pl.ds(0, 3 * sites)
    imag = pl.ds(3 * sites, 3 * sites)
    for index in range(2):
        packed = packed_elemental(
            w_ref[index, real, :].astype(BF16),
            w_ref[index, imag, :].astype(BF16),
            v_ref[real, :],
            v_ref[imag, :],
        )
        o_ref[pl.ds(index * vectors, vectors), :] = packed.astype(BF16)


def rotated(half, field, w_ref):
    columns = dot(identity(half), field[6 * half :, :half], 1, 1)
    vec = [field[comp * half : (comp + 1) * half, :].astype(F32) for comp in range(6)]
    for comp, value in enumerate(adjoint_product(columns, 0, vec)):
        w_ref[pl.ds(comp * half, half), :] = value.astype(w_ref.dtype)


def early_kernel(half, own_ref, along_ref, w_ref):
    even = lax.rem(lax.axis_index("space"), 2) == 0
    rotated(half, jnp.where(even, own_ref[...], along_ref[...]), w_ref)


def late_kernel(half, early_ref, own_ref, across_ref, along_ref, flat_ref, *rest):
    chunks, w_ref, y_ref = rest[:-2], rest[-2], rest[-1]
    near = len(chunks)
    even = lax.rem(lax.axis_index("space"), 2) == 0
    rotated(half, across_ref[...], w_ref)
    real, imag = pl.ds(0, 3 * half), pl.ds(3 * half, 3 * half)
    packed = packed_elemental(
        early_ref[real, :], early_ref[imag, :], across_ref[real, :], across_ref[imag, :]
    ) + packed_elemental(
        w_ref[real, :].astype(BF16),
        w_ref[imag, :].astype(BF16),
        jnp.where(even, along_ref[real, :], own_ref[real, :]),
        jnp.where(even, along_ref[imag, :], own_ref[imag, :]),
    )
    y_ref[...] = packed.astype(BF16)
    place = lax.rem(lax.axis_index("space"), near)
    wide, narrow = flat_ref.shape[0] // near, y_ref.shape[0] // near
    for partner, chunk_ref in enumerate(chunks):
        chunk = jnp.bitwise_xor(place, partner)
        chunk_ref[pl.ds(0, wide), :] = flat_ref[pl.ds(pl.multiple_of(chunk * wide, wide), wide), :]
        chunk_ref[pl.ds(wide, narrow), :] = y_ref[
            pl.ds(pl.multiple_of(chunk * narrow, narrow), narrow), :
        ]


def spread(size):
    rows = lax.broadcasted_iota(jnp.int32, (SPIN * size, SPIN * size), 0)
    cols = lax.broadcasted_iota(jnp.int32, (SPIN * size, SPIN * size), 1)
    target = (rows % size) * SPIN + rows // size
    return jnp.where(cols == target, 1.0, 0.0).astype(BF16)


def spins_kernel(p_ref, minus_ref, plus_ref, s_ref):
    columns, wide = p_ref.shape[1], p_ref.shape[2]
    vectors = wide // SPIN
    block = 128
    table = spread(block)
    s_ref[...] = spread(s_ref.shape[0] // SPIN)
    for chunk in range(vectors // block):
        at = pl.ds(chunk * block * SPIN, block * SPIN)
        real = dot(p_ref[0, :, at], table, 1, 1)
        imag = dot(p_ref[1, :, at], table, 1, 1)
        less = (0.5 * (real - imag)).astype(BF16)
        more = (0.5 * (real + imag)).astype(BF16)
        to = pl.ds(chunk * block, block)
        for spin in range(SPIN):
            lanes = slice(spin * block, (spin + 1) * block)
            rows = pl.ds(2 * spin * columns, columns)
            below = pl.ds((2 * spin + 1) * columns, columns)
            minus_ref[rows, to] = less[:, lanes]
            minus_ref[below, to] = more[:, lanes]
            plus_ref[rows, to] = -more[:, lanes]
            plus_ref[below, to] = less[:, lanes]


def last_kernel(near, dirs_ref, *refs):
    chunks = refs[:near]
    minus_ref, plus_ref, s_ref, o_ref, flat_ref, y_ref, product_ref, whole_ref, sems = refs[near:]
    vectors = y_ref.shape[0]
    columns = o_ref.shape[2]
    block = s_ref.shape[0] // SPIN
    place = lax.rem(lax.axis_index("space"), near)
    wide, narrow = 2 * vectors // near, vectors // near
    for partner, chunk_ref in enumerate(chunks):
        chunk = jnp.bitwise_xor(place, partner)
        flat_ref[pl.ds(pl.multiple_of(chunk * wide, wide), wide), :] = chunk_ref[pl.ds(0, wide), :]
        y_ref[pl.ds(pl.multiple_of(chunk * narrow, narrow), narrow), :] = chunk_ref[
            pl.ds(wide, narrow), :
        ]
    copies = []

    def multiply(direction):
        if direction == 1:
            packed = y_ref[...]
        else:
            packed = flat_ref[pl.ds(direction // 2 * vectors, vectors), :]
        step = 4 * columns
        for first in range(0, 2 * SPIN * columns, step):
            rows = pl.ds(first, step)
            product_ref[direction, rows, :] = (
                dot(minus_ref[rows, :], packed, 1, 1) + dot(plus_ref[rows, :], packed, 1, 0)
            ).astype(BF16)

    def store(direction):
        to_place = jnp.where(dirs_ref[1] == direction, 1, jnp.where(dirs_ref[2] == direction, 2, 0))
        for chunk in range(vectors // block):
            piece = jnp.concatenate(
                [
                    product_ref[
                        direction,
                        pl.ds(2 * spin * columns, 2 * columns),
                        pl.ds(chunk * block, block),
                    ]
                    for spin in range(SPIN)
                ],
                axis=1,
            )
            apart = dot(piece, s_ref[...], 1, 0).astype(BF16)
            to = pl.ds(chunk * block * SPIN, block * SPIN)
            whole_ref[direction, 0, :, to] = apart[:columns]
            whole_ref[direction, 1, :, to] = apart[columns:]
            copy = pltpu.make_async_copy(
                whole_ref.at[direction, :, :, to],
                o_ref.at[to_place, :, :, to],
                sems.at[direction, chunk],
            )
            copy.start()
            copies.append(copy)

    multiply(0)
    multiply(2)
    store(0)
    multiply(1)
    store(2)
    store(1)
    for copy in copies:
        copy.wait()


def last_call(dirs, chunks, minus, plus, table, shape):
    near = len(chunks)
    vectors = chunks[0].shape[1]
    return pl.pallas_call(
        functools.partial(last_kernel, near),
        in_specs=[pl.BlockSpec(memory_space=pltpu.SMEM)] + [VMEM] * (near + 3),
        out_specs=HBM,
        out_shape=jax.ShapeDtypeStruct(shape, BF16),
        scratch_shapes=[
            pltpu.VMEM((2 * vectors, vectors), BF16),
            pltpu.VMEM((vectors, vectors), BF16),
            pltpu.VMEM((shape[0],) + minus.shape, BF16),
            pltpu.VMEM(shape, BF16),
            pltpu.SemaphoreType.DMA((shape[0], vectors * SPIN // table.shape[0])),
        ],
        cost_estimate=pl.CostEstimate(
            flops=2_400_000_000, bytes_accessed=3_000_000, transcendentals=0
        ),
        compiler_params=pltpu.CompilerParams(vmem_limit_bytes=12 * 1024 * 1024),
    )(dirs, *chunks, minus, plus, table)


def swap(block, ranks, distance):
    return lax.ppermute(block, "space", [(i, i ^ distance) for i in range(ranks)])


def sum_over_space(chunks, ranks):
    near = len(chunks)
    total = chunks[0].astype(F32)
    for partner in range(near - 1, 0, -1):
        total = total + swap(chunks[partner], ranks, partner).astype(F32)
    stride = near
    while stride < ranks:
        total = total + swap(total.astype(BF16), ranks, stride).astype(F32)
        stride *= 2
    whole = [total.astype(BF16)]
    for partner in range(1, near):
        whole.append(swap(whole[0], ranks, partner))
    return whole


def blocks(eigvecs, links, dirs, peram):
    ranks = lax.axis_size("space")
    vectors, sites = eigvecs.shape[2], eigvecs.shape[4]
    assert sites == LX * LZ and ranks % 2 == 0
    field = jnp.transpose(eigvecs[0], (0, 2, 3, 1)).reshape(6 * sites, vectors)
    link_rows = links[0].reshape(27, 2, sites)
    half = half_rows(sites)
    rows = 6 * half + padded(18)
    near = 4 if ranks % 4 == 0 else 2

    payload = pltpu.VMEM((rows, vectors), BF16)
    across, along = pl.pallas_call(
        functools.partial(prepare_kernel, sites),
        out_shape=(payload, payload),
        in_specs=[HBM, HBM],
        out_specs=(VMEM, VMEM),
        scratch_shapes=[
            pltpu.VMEM((9, 2, sites), BF16),
            pltpu.SemaphoreType.DMA((2, 6)),
            pltpu.SemaphoreType.DMA,
        ],
        compiler_params=pltpu.CompilerParams(vmem_limit_bytes=VMEM_BYTES - 4 * rows * vectors),
    )(field, link_rows)
    from_across = lax.ppermute(across, "space", [(i, i ^ 1) for i in range(ranks)])
    from_along = lax.ppermute(
        along,
        "space",
        [((i + 2) % ranks if i % 2 == 0 else (i - 2) % ranks, i) for i in range(ranks)],
    )
    partner = lax.ppermute(peram[0], "tm", [((i + 1) % 2, i) for i in range(2)])

    flat = pl.pallas_call(
        functools.partial(front_kernel, sites),
        out_shape=jax.ShapeDtypeStruct((2 * vectors, vectors), BF16),
        in_specs=[VMEM] * 2,
        out_specs=VMEM,
        scratch_shapes=[pltpu.VMEM((2, 6 * sites, vectors), F32)],
        cost_estimate=pl.CostEstimate(flops=700_000_000, bytes_accessed=8_000_000, transcendentals=0),
        compiler_params=PARAMS,
    )(field, link_rows)
    columns = partner.shape[1]
    minus, plus, table = pl.pallas_call(
        spins_kernel,
        out_shape=(
            jax.ShapeDtypeStruct((2 * SPIN * columns, vectors), BF16),
            jax.ShapeDtypeStruct((2 * SPIN * columns, vectors), BF16),
            jax.ShapeDtypeStruct((SPIN * 64, SPIN * 64), BF16),
        ),
        in_specs=[VMEM],
        out_specs=(VMEM, VMEM, VMEM),
        cost_estimate=pl.CostEstimate(flops=500_000_000, bytes_accessed=2_000_000, transcendentals=0),
        compiler_params=PARAMS,
    )(partner)
    early = pl.pallas_call(
        functools.partial(early_kernel, half),
        out_shape=jax.ShapeDtypeStruct((6 * half, vectors), BF16),
        in_specs=[VMEM] * 2,
        out_specs=VMEM,
        cost_estimate=pl.CostEstimate(
            flops=20_000_000, bytes_accessed=1_000_000, transcendentals=0
        ),
        compiler_params=PARAMS,
    )(along, from_along)
    chunks = pl.pallas_call(
        functools.partial(late_kernel, half),
        out_shape=[jax.ShapeDtypeStruct((3 * vectors // near, vectors), BF16)] * near,
        in_specs=[VMEM] * 5,
        out_specs=[VMEM] * near,
        scratch_shapes=[pltpu.VMEM((6 * half, vectors), F32), pltpu.VMEM((vectors, vectors), BF16)],
        cost_estimate=pl.CostEstimate(
            flops=400_000_000, bytes_accessed=2_000_000, transcendentals=0
        ),
        compiler_params=PARAMS,
    )(early, along, from_across, from_along, flat)
    chunks = sum_over_space(chunks, ranks)
    shape = (dirs.shape[0], 2, columns, SPIN * vectors)
    result = last_call(dirs, chunks, minus, plus, table, shape)
    return result[None]


def solution(mesh):
    placed = (
        P(("parts", "tm"), None, None, None, "space"),
        P(("parts", "tm"), None, None, None, None, "space"),
        P(),
        P(("parts", "tm"), None, "space", None),
    )
    return jax.shard_map(
        blocks,
        mesh=mesh,
        in_specs=placed,
        out_specs=P(("parts", "tm"), None, None, "space", None),
        check_vma=False,
    )
```

```python
import functools

import jax
import jax.numpy as jnp
from jax import lax
from jax.experimental import pallas as pl
from jax.experimental.pallas import tpu as pltpu
from jax.sharding import PartitionSpec as P


SPIN = 4
LX = 9
LZ = 24
F32 = jnp.float32
BF16 = jnp.bfloat16
VMEM = pl.BlockSpec(memory_space=pltpu.VMEM)
ANY = pl.BlockSpec(memory_space=pl.ANY)
HBM = pl.BlockSpec(memory_space=pltpu.HBM)
VMEM_BYTES = 67_043_328
PARAMS = pltpu.CompilerParams(vmem_limit_bytes=12 * 1024 * 1024)


def half_rows(sites):
    return 8 * ((sites + 15) // 16)


def padded(count):
    return 8 * ((count + 7) // 8)


def identity(size):
    rows = lax.broadcasted_iota(jnp.int32, (size, size), 0)
    cols = lax.broadcasted_iota(jnp.int32, (size, size), 1)
    return jnp.where(rows == cols, 1.0, 0.0).astype(BF16)


def dot(left, right, left_dim, right_dim):
    return lax.dot_general(
        left, right, (((left_dim,), (right_dim,)), ((), ())), preferred_element_type=F32
    )


def adjoint_product(columns, base, vec):
    real_rows, imag_rows = [], []
    for out in range(3):
        real_sum = imag_sum = None
        for inner in range(3):
            at = base + (inner * 3 + out) * 2
            link_real = columns[:, at : at + 1]
            link_imag = columns[:, at + 1 : at + 2]
            real = link_real * vec[inner] + link_imag * vec[3 + inner]
            imag = link_real * vec[3 + inner] - link_imag * vec[inner]
            real_sum = real if real_sum is None else real_sum + real
            imag_sum = imag if imag_sum is None else imag_sum + imag
        real_rows.append(real_sum)
        imag_rows.append(imag_sum)
    return real_rows + imag_rows


def packed_elemental(w_real, w_imag, v_real, v_imag):
    real = dot(w_real, v_real, 0, 0) + dot(w_imag, v_imag, 0, 0)
    imag = dot(w_real, v_imag, 0, 0) - dot(w_imag, v_real, 0, 0)
    return (real + imag) + jnp.transpose(imag - real)


def link_table(u_ref, first, last):
    return jnp.concatenate([u_ref[at].astype(F32) for at in range(first, last)], axis=0)


def prepare_kernel(sites, v_ref, u_ref, across_ref, along_ref, link_ref, sems, link_sem):
    half = half_rows(sites)
    overlap = 2 * half - sites
    vectors = v_ref.shape[1]
    parity = lax.rem(lax.axis_index("space"), 2)
    fetch = pltpu.make_async_copy(u_ref.at[pl.ds(9, 9)], link_ref, link_sem)
    fetch.start()
    copies = []
    for slot, (ref, upper) in enumerate(((across_ref, 1 - parity), (along_ref, parity))):
        for comp in range(6):
            first = pl.multiple_of(comp * sites + upper * (sites - half), 8)
            copy = pltpu.make_async_copy(
                v_ref.at[pl.ds(first, half)],
                ref.at[pl.ds(comp * half, half)],
                sems.at[slot, comp],
            )
            copy.start()
            copies.append(copy)
    fetch.wait()
    links = link_table(link_ref, 0, 9)
    rows = across_ref.shape[0] - 6 * half
    lower = links[:, :half]
    upper = links[:, sites - half :]
    lane = lax.broadcasted_iota(jnp.int32, upper.shape, 1)
    upper = jnp.where(lane < overlap, 0.0, upper)
    for ref, wanted in ((across_ref, 1 - parity), (along_ref, parity)):
        block = jnp.where(wanted == 1, upper, lower)
        block = jnp.concatenate([block, jnp.zeros((rows - block.shape[0], half), F32)], axis=0)
        block = jnp.concatenate([block, jnp.zeros((rows, vectors - half), F32)], axis=1)
        ref[pl.ds(6 * half, rows), :] = block.astype(BF16)
    for copy in copies:
        copy.wait()


def front_kernel(sites, v_ref, u_ref, o_ref, w_ref):
    planes = sites // LZ
    vectors = v_ref.shape[1]
    columns = dot(identity(sites), link_table(u_ref, 0, 27).astype(BF16), 1, 1)
    for plane in range(planes):
        slab, along = plane // LX, plane % LX
        start = plane * LZ
        vec = [v_ref[pl.ds(comp * sites + start, LZ), :].astype(F32) for comp in range(6)]
        here = columns[start : start + LZ, :]
        ahead = (slab * LX + (along + 1) % LX) * LZ
        for comp, value in enumerate(adjoint_product(here, 0, vec)):
            w_ref[0, pl.ds(comp * sites + ahead, LZ), :] = value
        for comp, value in enumerate(adjoint_product(here, 36, vec)):
            w_ref[1, pl.ds(comp * sites + start, LZ), :] = pltpu.roll(value, 1, 0)
    real = pl.ds(0, 3 * sites)
    imag = pl.ds(3 * sites, 3 * sites)
    for index in range(2):
        packed = packed_elemental(
            w_ref[index, real, :].astype(BF16),
            w_ref[index, imag, :].astype(BF16),
            v_ref[real, :],
            v_ref[imag, :],
        )
        o_ref[pl.ds(index * vectors, vectors), :] = packed.astype(BF16)


def rotated(half, field, w_ref):
    columns = dot(identity(half), field[6 * half :, :half], 1, 1)
    vec = [field[comp * half : (comp + 1) * half, :].astype(F32) for comp in range(6)]
    for comp, value in enumerate(adjoint_product(columns, 0, vec)):
        w_ref[pl.ds(comp * half, half), :] = value.astype(w_ref.dtype)


def early_kernel(half, own_ref, along_ref, w_ref):
    even = lax.rem(lax.axis_index("space"), 2) == 0
    rotated(half, jnp.where(even, own_ref[...], along_ref[...]), w_ref)


def late_kernel(half, early_ref, own_ref, across_ref, along_ref, flat_ref, *rest):
    chunks, w_ref, y_ref = rest[:-2], rest[-2], rest[-1]
    near = len(chunks)
    even = lax.rem(lax.axis_index("space"), 2) == 0
    rotated(half, across_ref[...], w_ref)
    real, imag = pl.ds(0, 3 * half), pl.ds(3 * half, 3 * half)
    left = jnp.concatenate(
        [early_ref[real, :], early_ref[imag, :], w_ref[real, :], w_ref[imag, :]], axis=0
    )
    own_real = jnp.where(even, along_ref[real, :], own_ref[real, :])
    own_imag = jnp.where(even, along_ref[imag, :], own_ref[imag, :])
    v_real, v_imag = across_ref[real, :], across_ref[imag, :]
    re = dot(left, jnp.concatenate([v_real, v_imag, own_real, own_imag], axis=0), 0, 0)
    im = dot(left, jnp.concatenate([v_imag, -v_real, own_imag, -own_real], axis=0), 0, 0)
    packed = (re + im) + jnp.transpose(im - re)
    y_ref[...] = packed.astype(BF16)
    place = lax.rem(lax.axis_index("space"), near)
    wide, narrow = flat_ref.shape[0] // near, y_ref.shape[0] // near
    for partner, chunk_ref in enumerate(chunks):
        chunk = jnp.bitwise_xor(place, partner)
        chunk_ref[pl.ds(0, wide), :] = flat_ref[pl.ds(pl.multiple_of(chunk * wide, wide), wide), :]
        chunk_ref[pl.ds(wide, narrow), :] = y_ref[
            pl.ds(pl.multiple_of(chunk * narrow, narrow), narrow), :
        ]


def spread(size):
    rows = lax.broadcasted_iota(jnp.int32, (SPIN * size, SPIN * size), 0)
    cols = lax.broadcasted_iota(jnp.int32, (SPIN * size, SPIN * size), 1)
    target = (rows % size) * SPIN + rows // size
    return jnp.where(cols == target, 1.0, 0.0).astype(BF16)


def spins_kernel(p_ref, minus_ref, plus_ref, s_ref):
    columns, wide = p_ref.shape[1], p_ref.shape[2]
    vectors = wide // SPIN
    block = 128
    table = spread(block)
    s_ref[...] = spread(s_ref.shape[0] // SPIN)
    for chunk in range(vectors // block):
        at = pl.ds(chunk * block * SPIN, block * SPIN)
        real = dot(p_ref[0, :, at], table, 1, 1)
        imag = dot(p_ref[1, :, at], table, 1, 1)
        less = (0.5 * (real - imag)).astype(BF16)
        more = (0.5 * (real + imag)).astype(BF16)
        to = pl.ds(chunk * block, block)
        for spin in range(SPIN):
            lanes = slice(spin * block, (spin + 1) * block)
            rows = pl.ds(2 * spin * columns, columns)
            below = pl.ds((2 * spin + 1) * columns, columns)
            minus_ref[rows, to] = less[:, lanes]
            minus_ref[below, to] = more[:, lanes]
            plus_ref[rows, to] = -more[:, lanes]
            plus_ref[below, to] = less[:, lanes]


def last_kernel(near, dirs_ref, *refs):
    chunks = refs[:near]
    minus_ref, plus_ref, s_ref, o_ref, flat_ref, y_ref, product_ref, whole_ref, sems = refs[near:]
    vectors = y_ref.shape[0]
    columns = o_ref.shape[2]
    block = s_ref.shape[0] // SPIN
    place = lax.rem(lax.axis_index("space"), near)
    wide, narrow = 2 * vectors // near, vectors // near
    for partner, chunk_ref in enumerate(chunks):
        chunk = jnp.bitwise_xor(place, partner)
        flat_ref[pl.ds(pl.multiple_of(chunk * wide, wide), wide), :] = chunk_ref[pl.ds(0, wide), :]
        y_ref[pl.ds(pl.multiple_of(chunk * narrow, narrow), narrow), :] = chunk_ref[
            pl.ds(wide, narrow), :
        ]
    copies = []

    def multiply(direction):
        if direction == 1:
            packed = y_ref[...]
        else:
            packed = flat_ref[pl.ds(direction // 2 * vectors, vectors), :]
        step = 4 * columns
        for first in range(0, 2 * SPIN * columns, step):
            rows = pl.ds(first, step)
            product_ref[direction, rows, :] = (
                dot(minus_ref[rows, :], packed, 1, 1) + dot(plus_ref[rows, :], packed, 1, 0)
            ).astype(BF16)

    def store(direction):
        to_place = jnp.where(dirs_ref[1] == direction, 1, jnp.where(dirs_ref[2] == direction, 2, 0))
        for chunk in range(vectors // block):
            piece = jnp.concatenate(
                [
                    product_ref[
                        direction,
                        pl.ds(2 * spin * columns, 2 * columns),
                        pl.ds(chunk * block, block),
                    ]
                    for spin in range(SPIN)
                ],
                axis=1,
            )
            apart = dot(piece, s_ref[...], 1, 0).astype(BF16)
            to = pl.ds(chunk * block * SPIN, block * SPIN)
            whole_ref[direction, 0, :, to] = apart[:columns]
            whole_ref[direction, 1, :, to] = apart[columns:]
            copy = pltpu.make_async_copy(
                whole_ref.at[direction, :, :, to],
                o_ref.at[to_place, :, :, to],
                sems.at[direction, chunk],
            )
            copy.start()
            copies.append(copy)

    multiply(0)
    multiply(2)
    store(0)
    multiply(1)
    store(2)
    store(1)
    for copy in copies:
        copy.wait()


def last_call(dirs, chunks, minus, plus, table, shape):
    near = len(chunks)
    vectors = chunks[0].shape[1]
    return pl.pallas_call(
        functools.partial(last_kernel, near),
        in_specs=[pl.BlockSpec(memory_space=pltpu.SMEM)] + [VMEM] * (near + 3),
        out_specs=HBM,
        out_shape=jax.ShapeDtypeStruct(shape, BF16),
        scratch_shapes=[
            pltpu.VMEM((2 * vectors, vectors), BF16),
            pltpu.VMEM((vectors, vectors), BF16),
            pltpu.VMEM((shape[0],) + minus.shape, BF16),
            pltpu.VMEM(shape, BF16),
            pltpu.SemaphoreType.DMA((shape[0], vectors * SPIN // table.shape[0])),
        ],
        cost_estimate=pl.CostEstimate(
            flops=2_400_000_000, bytes_accessed=3_000_000, transcendentals=0
        ),
        compiler_params=pltpu.CompilerParams(vmem_limit_bytes=12 * 1024 * 1024),
    )(dirs, *chunks, minus, plus, table)


def swap(block, ranks, distance):
    return lax.ppermute(block, "space", [(i, i ^ distance) for i in range(ranks)])


def sum_over_space(chunks, ranks):
    near = len(chunks)
    total = chunks[0].astype(F32)
    for partner in range(near - 1, 0, -1):
        total = total + swap(chunks[partner], ranks, partner).astype(F32)
    stride = near
    while stride < ranks:
        total = total + swap(total.astype(BF16), ranks, stride).astype(F32)
        stride *= 2
    whole = [total.astype(BF16)]
    for partner in range(1, near):
        whole.append(swap(whole[0], ranks, partner))
    return whole


def blocks(eigvecs, links, dirs, peram):
    ranks = lax.axis_size("space")
    vectors, sites = eigvecs.shape[2], eigvecs.shape[4]
    assert sites == LX * LZ and ranks % 2 == 0
    field = jnp.transpose(eigvecs[0], (0, 2, 3, 1)).reshape(6 * sites, vectors)
    link_rows = links[0].reshape(27, 2, sites)
    half = half_rows(sites)
    rows = 6 * half + padded(18)
    near = 4 if ranks % 4 == 0 else 2

    payload = pltpu.VMEM((rows, vectors), BF16)
    across, along = pl.pallas_call(
        functools.partial(prepare_kernel, sites),
        out_shape=(payload, payload),
        in_specs=[HBM, HBM],
        out_specs=(VMEM, VMEM),
        scratch_shapes=[
            pltpu.VMEM((9, 2, sites), BF16),
            pltpu.SemaphoreType.DMA((2, 6)),
            pltpu.SemaphoreType.DMA,
        ],
        compiler_params=pltpu.CompilerParams(vmem_limit_bytes=VMEM_BYTES - 4 * rows * vectors),
    )(field, link_rows)
    from_across = lax.ppermute(across, "space", [(i, i ^ 1) for i in range(ranks)])
    from_along = lax.ppermute(
        along,
        "space",
        [((i + 2) % ranks if i % 2 == 0 else (i - 2) % ranks, i) for i in range(ranks)],
    )
    partner = lax.ppermute(peram[0], "tm", [((i + 1) % 2, i) for i in range(2)])

    flat = pl.pallas_call(
        functools.partial(front_kernel, sites),
        out_shape=jax.ShapeDtypeStruct((2 * vectors, vectors), BF16),
        in_specs=[VMEM] * 2,
        out_specs=VMEM,
        scratch_shapes=[pltpu.VMEM((2, 6 * sites, vectors), F32)],
        cost_estimate=pl.CostEstimate(flops=700_000_000, bytes_accessed=8_000_000, transcendentals=0),
        compiler_params=PARAMS,
    )(field, link_rows)
    columns = partner.shape[1]
    minus, plus, table = pl.pallas_call(
        spins_kernel,
        out_shape=(
            jax.ShapeDtypeStruct((2 * SPIN * columns, vectors), BF16),
            jax.ShapeDtypeStruct((2 * SPIN * columns, vectors), BF16),
            jax.ShapeDtypeStruct((SPIN * 64, SPIN * 64), BF16),
        ),
        in_specs=[VMEM],
        out_specs=(VMEM, VMEM, VMEM),
        cost_estimate=pl.CostEstimate(flops=500_000_000, bytes_accessed=2_000_000, transcendentals=0),
        compiler_params=PARAMS,
    )(partner)
    early = pl.pallas_call(
        functools.partial(early_kernel, half),
        out_shape=jax.ShapeDtypeStruct((6 * half, vectors), BF16),
        in_specs=[VMEM] * 2,
        out_specs=VMEM,
        cost_estimate=pl.CostEstimate(
            flops=20_000_000, bytes_accessed=1_000_000, transcendentals=0
        ),
        compiler_params=PARAMS,
    )(along, from_along)
    chunks = pl.pallas_call(
        functools.partial(late_kernel, half),
        out_shape=[jax.ShapeDtypeStruct((3 * vectors // near, vectors), BF16)] * near,
        in_specs=[VMEM] * 5,
        out_specs=[VMEM] * near,
        scratch_shapes=[
            pltpu.VMEM((6 * half, vectors), BF16),
            pltpu.VMEM((vectors, vectors), BF16),
        ],
        cost_estimate=pl.CostEstimate(
            flops=400_000_000, bytes_accessed=2_000_000, transcendentals=0
        ),
        compiler_params=PARAMS,
    )(early, along, from_across, from_along, flat)
    chunks = sum_over_space(chunks, ranks)
    shape = (dirs.shape[0], 2, columns, SPIN * vectors)
    result = last_call(dirs, chunks, minus, plus, table, shape)
    return result[None]


def solution(mesh):
    placed = (
        P(("parts", "tm"), None, None, None, "space"),
        P(("parts", "tm"), None, None, None, None, "space"),
        P(),
        P(("parts", "tm"), None, "space", None),
    )
    return jax.shard_map(
        blocks,
        mesh=mesh,
        in_specs=placed,
        out_specs=P(("parts", "tm"), None, None, "space", None),
        check_vma=False,
    )
```
